256 devices in a mesh: cells: 16 (over x, z_hi), vel: 16 (over y, z_lo, core).
Axes of the slice: x: 4, y: 4, z: 8 (z_hi: 4, z_lo: 2; z = z_hi * 2 + z_lo), core: 2. Of those that a mesh axis runs over, the one named last changes fastest.
Arguments:
- dist: float32 [32768, 64, 128], P('vel', 'cells'), may hold values from 0.05 to 2
- basis: float32 [512, 32768], P(None, 'vel'), may hold values from -0.03125 to 0.03125
- left_factor: float32 [2048, 512], P('vel'), may hold values from -0.25 to 0.25
- right_factor: float32 [2048, 512], P('vel'), may hold values from -0.25 to 0.25
- mixing: float32 [512, 2048], P(None, 'vel'), may hold values from -0.125 to 0.125
- next_cell: int32 [64, 128], P('cells'), may hold values from 0 to 127, as said below
- prev_cell: int32 [64, 128], P('cells'), may hold values from 0 to 127, as said below
- cell_kind: int32 [64, 128], P('cells'), may hold values 0 or 1
Outputs:
- relaxed: float32 [32768, 64, 128], P('vel', 'cells')
The draws below stay inside these ranges and needn't reach their ends.
Inputs may be any that keep to these rules, and one draw needn't show every extreme that they name: In each column x, following next_cell[x, y] from any row visits all 128 rows once before returning. prev_cell[x, next_cell[x, y]] = y for every cell.
All inputs are finite; a program needn't handle non-finite values. No bound on the sum of `cell_kind` on one device may be relied on, other than what follows from the above.
Results may differ from the reference program's by a relative error of at most 0.0003.
Values sent between devices are 32-bit elements; how exact they have to be, the bound alone decides.
No kernel may reach another device: no remote copies, remote signals or barrier semaphores. Data moves between devices by JAX's collectives and lax.ppermute only.
A program may use at most 64 MiB of HBM per device.

```python
import math
import jax
import jax.numpy as jnp
from jax import lax

NV1 = 32
K = 512
R = 2048
TY = 128
V = 32768
NX = 64
N_VEL = 16


def cycle_tables(key):
    base = jax.random.fold_in(key, 11)
    keys = jax.random.split(base, NX)
    orders = jax.vmap(lambda single: jax.random.permutation(single, TY))(keys).astype(jnp.int32)
    columns = jnp.broadcast_to(jnp.arange(NX, dtype=jnp.int32)[:, None], (NX, TY))
    following = jnp.roll(orders, -1, axis=1)
    preceding = jnp.roll(orders, 1, axis=1)
    forward = jnp.zeros((NX, TY), jnp.int32).at[columns, orders].set(following)
    backward = jnp.zeros((NX, TY), jnp.int32).at[columns, orders].set(preceding)
    return (forward, backward)


def draw_next_cell(key, part):
    return cycle_tables(key)[0]


def draw_prev_cell(key, part):
    return cycle_tables(key)[1]


def touch_ends(entries, rng, smallest, top_value):
    index_at = [jax.random.randint(jax.random.fold_in(rng, axis), (), 0, length) for axis, length in enumerate(entries.shape)]
    widest = entries.shape.index(max(entries.shape))
    next_to = index_at[:widest] + [(index_at[widest] + 1) % entries.shape[widest]] + index_at[widest + 1:]
    return entries.at[tuple(index_at)].set(smallest).at[tuple(next_to)].set(top_value)


def levels(rng, dims, pieces, low, largest):
    level = 1.0
    for axis_at, shards_of in pieces:
        steps = jax.random.uniform(jax.random.fold_in(jax.random.fold_in(rng, 6), axis_at), (shards_of,), jnp.float32, low / len(pieces), largest / len(pieces))
        level = level * jnp.repeat(jnp.exp(steps), dims[axis_at] // shards_of).reshape((-1,) + (1,) * (len(dims) - 1 - axis_at))
    return level


def bell_draw(own_key, shape, deviation, most, pieces=(), held_as=jnp.bfloat16):
    level = levels(own_key, shape, pieces, -0.22, 0.18) if pieces else 1.0
    values = jax.random.normal(own_key, shape, jnp.float32) * deviation * level
    return jnp.minimum(jnp.maximum(values, -most), most).astype(held_as)


def setup_inputs(seed: int = 0) -> dict:
    splits = jax.random.split(jax.random.key(seed), 9)
    return {
        "dist": jnp.clip(jnp.exp(math.log(2.0) - 3.6888794 * jax.random.uniform(splits[0], (V, NX, TY), jnp.float32) ** levels(splits[0], (V, NX, TY), ((0, 16), (1, 16)), -0.2, 0.2)), 0.05, 2.0),
        "basis": bell_draw(splits[1], (K, V), V ** -0.5, 0.03125, ((1, 16),), jnp.float32),
        "left_factor": bell_draw(splits[2], (R, K), K ** -0.5, 0.25, ((0, 16),), jnp.float32),
        "right_factor": bell_draw(splits[3], (R, K), K ** -0.5, 0.25, ((0, 16),), jnp.float32),
        "mixing": bell_draw(splits[4], (K, R), R ** -0.5, 0.125, ((1, 16),), jnp.float32),
        "next_cell": draw_next_cell(jax.random.fold_in(splits[8], 71), 0),
        "prev_cell": draw_prev_cell(jax.random.fold_in(splits[8], 71), 0),
        "cell_kind": touch_ends((jax.random.randint(splits[7], (NX, TY), 0, 6) < 1).astype(jnp.int32), jax.random.fold_in(splits[7], 1), 0, 1),
    }


SPEED_RANGE = 6.4
RATIO_X = 0.2
RATIO_Y = 0.12
HALF_STEP = 0.5


def minmod(first, second):
    return 0.5 * (jnp.sign(first) + jnp.sign(second)) * jnp.minimum(jnp.abs(first), jnp.abs(second))


def face_flux(upwind, behind, ahead, courant):
    return courant * (upwind + 0.5 * (1.0 - jnp.abs(courant)) * minmod(upwind - behind, ahead - upwind))


def components(grid_index, points):
    plane = points * points
    index_x = grid_index // plane
    index_y = (grid_index // points) % points
    step = SPEED_RANGE / points
    middle = (points - 1) * 0.5
    return (index_x.astype(jnp.float32) - middle) * step, (index_y.astype(jnp.float32) - middle) * step


def x_divergence(padded, courant):
    width = padded.shape[1] - 4
    speed = courant[:, None, None]
    forward = face_flux(padded[:, 1:width + 2], padded[:, 0:width + 1], padded[:, 2:width + 3], speed)
    backward = face_flux(padded[:, 2:width + 3], padded[:, 3:width + 4], padded[:, 1:width + 2], speed)
    flux = jnp.where(speed > 0, forward, backward)
    return flux[:, 1:] - flux[:, :-1]


def pick_rows(values, index):
    return jnp.take_along_axis(values, jnp.broadcast_to(index[None], values.shape), axis=2)


def y_divergence(field, courant, following, preceding):
    speed = courant[:, None, None]
    above = pick_rows(field, following)
    below = pick_rows(field, preceding)
    above_two = pick_rows(above, following)
    forward = face_flux(field, below, above, speed)
    backward = face_flux(above, above_two, field, speed)
    flux = jnp.where(speed > 0, forward, backward)
    return flux - pick_rows(flux, preceding)


def reference(dist, basis, left_factor, right_factor, mixing, next_cell, prev_cell, cell_kind):
    total, extent_x, extent_y = dist.shape
    per_device = total // N_VEL
    half = per_device // 2
    glob = jnp.arange(total, dtype=jnp.int32)
    owner = glob // per_device
    local = glob % per_device
    grid_index = jnp.where(local < half, owner * half + local, total - 1 - (owner * half + local - half))
    speed_x, speed_y = components(grid_index, NV1)
    courant_x = (speed_x * RATIO_X).reshape(N_VEL, per_device)
    courant_y = (speed_y * RATIO_Y).reshape(N_VEL, per_device)
    fluid = (1 - cell_kind).astype(jnp.float32)
    blocks = dist.reshape(N_VEL, per_device, extent_x, extent_y)
    basis_blocks = basis.reshape(basis.shape[0], N_VEL, per_device).transpose(1, 0, 2)

    def transported(block, cxb, cyb):
        padded = jnp.concatenate([block[:, -2:], block, block[:, :2]], axis=1)
        return block - fluid * (x_divergence(padded, cxb) + y_divergence(block, cyb, next_cell, prev_cell))

    def accumulate(carry, items):
        block, cxb, cyb, piece = items
        moved = transported(block, cxb, cyb).reshape(per_device, extent_x * extent_y)
        return carry + jnp.dot(piece, moved, precision=lax.Precision.HIGHEST, preferred_element_type=jnp.float32), None

    start = jnp.zeros((basis.shape[0], extent_x * extent_y), jnp.float32)
    moments, _ = lax.scan(accumulate, start, (blocks, courant_x, courant_y, basis_blocks))
    first = jnp.dot(left_factor, moments, precision=lax.Precision.HIGHEST, preferred_element_type=jnp.float32)
    second = jnp.dot(right_factor, moments, precision=lax.Precision.HIGHEST, preferred_element_type=jnp.float32)
    collision = jnp.dot(mixing, first * second, precision=lax.Precision.HIGHEST, preferred_element_type=jnp.float32)

    def rebuild(items):
        block, cxb, cyb, piece = items
        moved = transported(block, cxb, cyb)
        gain = jnp.dot(piece.T, collision, precision=lax.Precision.HIGHEST, preferred_element_type=jnp.float32)
        return moved + HALF_STEP * fluid * gain.reshape(moved.shape)

    relaxed = lax.map(rebuild, (blocks, courant_x, courant_y, basis_blocks))
    return relaxed.reshape(dist.shape)
```

```python
import functools

import jax
import jax.numpy as jnp
from jax import lax
from jax.experimental import pallas as pl
from jax.experimental.pallas import tpu as pltpu
from jax.sharding import PartitionSpec as P

POINTS = 32
STEP = 6.4 / POINTS
MIDDLE = (POINTS - 1) * 0.5
RATIO_X = 0.2
RATIO_Y = 0.12
HALF_STEP = 0.5

COLUMNS = 4
ROWS = 128
PER_DEVICE = 2048
HALF = PER_DEVICE // 2
CHUNK = 256
MOMENTS = 512
CELLS = COLUMNS * ROWS
RANKS = 1024
GROUP = CELLS // 8
F32 = jnp.float32
BF16 = jnp.bfloat16
VMEM_LIMIT = 28 << 20


def shifted(x, by):
    size = lax.axis_size("cells")
    return lax.ppermute(x, "cells", [(i, (i + by) % size) for i in range(size)])


def exchanged(x, bit):
    return lax.ppermute(x, "vel", [(i, i ^ bit) for i in range(16)])


def along_y(x, by):
    return lax.ppermute(x, "vel", [(i, (i + 4 * by) % 16) for i in range(16)])


def halves(x):
    high = x.astype(BF16)
    return high, (x - high.astype(F32)).astype(BF16)


def minmod(a, b):
    return jnp.maximum(jnp.minimum(a, b), 0.0) + jnp.minimum(jnp.maximum(a, b), 0.0)


def dot(a, b):
    return jnp.dot(a, b, preferred_element_type=F32)


def dot_nt(a, b):
    return lax.dot_general(a, b, (((1,), (1,)), ((), ())), preferred_element_type=F32)


def column(ref, x, count=CHUNK):
    return ref[pl.ds(x, count, stride=COLUMNS), :]


def params(limit=VMEM_LIMIT):
    return pltpu.CompilerParams(vmem_limit_bytes=limit)


VM = pl.BlockSpec(memory_space=pltpu.VMEM)
SM = pl.BlockSpec(memory_space=pltpu.SMEM)


def pack_kernel(lower, upper, right, left):
    right[0] = column(upper, 3)
    right[1] = column(upper, 2)
    right[2] = column(lower, 3)
    left[0] = column(lower, 0)
    left[1] = column(lower, 1)
    left[2] = column(upper, 0)


def pack(flat):
    steps = HALF // CHUNK
    rows = CHUNK * COLUMNS
    out = jax.ShapeDtypeStruct((3, HALF, ROWS), F32)
    spec = pl.BlockSpec((3, CHUNK, ROWS), lambda i: (0, i, 0))
    return pl.pallas_call(
        pack_kernel,
        name="pack",
        grid=(steps,),
        in_specs=[
            pl.BlockSpec((rows, ROWS), lambda i: (i, 0)),
            pl.BlockSpec((rows, ROWS), lambda i: (i + steps, 0)),
        ],
        out_specs=[spec, spec],
        out_shape=[out, out],
        compiler_params=params(),
    )(flat, flat)


def local_kernel(speed, dist, kind, tables, out):
    step = pl.program_id(0)
    in_upper = step >= HALF // CHUNK
    line = lax.broadcasted_iota(jnp.int32, (CHUNK, ROWS), 0) + step * CHUNK
    along = (line // POINTS) % POINTS
    along = jnp.where(in_upper, POINTS - 1 - along, along)
    courant_y = jnp.abs((along.astype(F32) - MIDDLE) * STEP * RATIO_Y)
    slope_y = 0.5 * (1.0 - courant_y)
    courant_x = speed[0]
    slope_x = 0.5 * (1.0 - courant_x)
    fields = []
    for x in range(COLUMNS):
        here = column(dist, x)
        both = dot(jnp.concatenate(halves(here), axis=1), tables[0, x])
        face = here + slope_y * minmod(here - both[:, :ROWS], both[:, ROWS:] - here)
        behind = dot(jnp.concatenate(halves(face), axis=1), tables[0, x, :, :ROWS])
        fields.append((here, courant_y * (face - behind)))

    def finish(order):
        here = [fields[x][0] for x in order]
        change = [fields[x][1] for x in order]
        fluid = [(1 - kind[x : x + 1, :]).astype(F32) for x in order]
        face_1 = courant_x * (here[1] + slope_x * minmod(here[1] - here[0], here[2] - here[1]))
        face_2 = courant_x * (here[2] + slope_x * minmod(here[2] - here[1], here[3] - here[2]))
        out[order[0]] = here[0] - fluid[0] * change[0]
        out[order[1]] = here[1] - fluid[1] * (change[1] + face_1)
        out[order[2]] = here[2] - fluid[2] * (change[2] + (face_2 - face_1))
        out[order[3]] = here[3] - fluid[3] * (change[3] - face_2)

    @pl.when(in_upper)
    def _():
        finish((0, 1, 2, 3))

    @pl.when(jnp.logical_not(in_upper))
    def _():
        finish((3, 2, 1, 0))


def local_part(speed, flat, kind, tables):
    steps = PER_DEVICE // CHUNK
    quarter = steps // 4

    def against(i):
        return jnp.where((i >= quarter) & (i < 3 * quarter), 0, 1)

    return pl.pallas_call(
        local_kernel,
        name="local_transport",
        grid=(steps,),
        in_specs=[
            SM,
            pl.BlockSpec((CHUNK * COLUMNS, ROWS), lambda i: (i, 0)),
            VM,
            pl.BlockSpec((1, COLUMNS, 2 * ROWS, 2 * ROWS), lambda i: (against(i), 0, 0, 0)),
        ],
        out_specs=pl.BlockSpec((COLUMNS, CHUNK, ROWS), lambda i: (0, i, 0)),
        out_shape=jax.ShapeDtypeStruct((COLUMNS, PER_DEVICE, ROWS), F32),
        compiler_params=params(),
        cost_estimate=pl.CostEstimate(flops=4 << 30, bytes_accessed=10 << 20, transcendentals=0),
    )(speed, flat, kind, tables)


def row_tables(following, preceding):
    rows = jnp.arange(ROWS, dtype=jnp.int32)[None, :, None]
    after = (rows == following[:, None, :]).astype(BF16)
    before = (rows == preceding[:, None, :]).astype(BF16)
    forward = jnp.concatenate([before, after], axis=2)
    backward = jnp.concatenate([after, before], axis=2)
    forward = jnp.concatenate([forward, forward], axis=1)
    backward = jnp.concatenate([backward, backward], axis=1)
    return jnp.stack([forward, backward])


def basis_kernel(basis, high, low, turned_high, turned_low):
    values = basis[...]
    high[...], low[...] = halves(values)
    turned_high[...], turned_low[...] = halves(values.T)


def split_basis(basis):
    width = 256
    flat = pl.BlockSpec((MOMENTS, width), lambda i: (0, i))
    turned = pl.BlockSpec((width, MOMENTS), lambda i: (i, 0))
    return pl.pallas_call(
        basis_kernel,
        name="split_basis",
        grid=(PER_DEVICE // width,),
        in_specs=[flat],
        out_specs=[flat, flat, turned, turned],
        out_shape=[jax.ShapeDtypeStruct((MOMENTS, PER_DEVICE), BF16)] * 2
        + [jax.ShapeDtypeStruct((PER_DEVICE, MOMENTS), BF16)] * 2,
        compiler_params=params(),
        cost_estimate=pl.CostEstimate(flops=1 << 24, bytes_accessed=12 << 20, transcendentals=0),
    )(basis)


def factor_kernel(factors, high, low):
    high[...], low[...] = halves(factors[0])


def split_factors(factors):
    count = RANKS // 128
    out = jax.ShapeDtypeStruct((3, RANKS, MOMENTS), BF16)
    spec = pl.BlockSpec((3, 128, MOMENTS), lambda i: (0, i, 0))
    return pl.pallas_call(
        factor_kernel,
        name="split_factors",
        grid=(count,),
        in_specs=[pl.BlockSpec((1, 3, 128, MOMENTS), lambda i: (i, 0, 0, 0))],
        out_specs=[spec, spec],
        out_shape=[out, out],
        compiler_params=params(),
        cost_estimate=pl.CostEstimate(flops=1 << 24, bytes_accessed=12 << 20, transcendentals=0),
    )(factors)


def moments_kernel(
    speed, place, lower, upper, part_lower, part_upper, from_left, from_right, kind,
    high_lower, low_lower, high_upper, low_upper,
    moved_lower, moved_upper, kept, sent, total,
):
    step = pl.program_id(0)
    courant = speed[0]
    slope = 0.5 * (1.0 - courant)

    def half(dist, part, moved, order, behind, behind_two, ahead):
        first, second = column(dist, order[0]), column(dist, order[1])
        third, fourth = column(dist, order[2]), column(dist, order[3])
        fluid = [courant * (1 - kind[x : x + 1, :]).astype(F32) for x in order]
        face_in = behind + slope * minmod(behind - behind_two, first - behind)
        face_0 = first + slope * minmod(first - behind, second - first)
        face_3 = fourth + slope * minmod(fourth - third, ahead - fourth)
        values = [None] * COLUMNS
        values[order[0]] = part[order[0]] - fluid[0] * (face_0 - face_in)
        values[order[1]] = part[order[1]] + fluid[1] * face_0
        values[order[2]] = part[order[2]]
        values[order[3]] = part[order[3]] - fluid[3] * face_3
        for x in range(COLUMNS):
            moved[x] = values[x]
        return halves(jnp.concatenate(values, axis=1))

    def share(high, low, values):
        top, rest = values
        return dot(high[...], top) + (dot(high[...], rest) + dot(low[...], top))

    values_lower = half(
        lower, part_lower, moved_lower, (3, 2, 1, 0), from_right[0], from_right[1], from_left[2]
    )
    values_upper = half(
        upper, part_upper, moved_upper, (0, 1, 2, 3), from_left[0], from_left[1], from_right[2]
    )
    added = share(high_lower, low_lower, values_lower) + share(high_upper, low_upper, values_upper)

    @pl.when(step == 0)
    def _():
        total[...] = added

    @pl.when(step > 0)
    def _():
        total[...] += added

    @pl.when(step == pl.num_programs(0) - 1)
    def _():
        count = CELLS // 2
        core = place[0]
        first = total[:, :count].T
        second = total[:, count:].T
        kept[...] = jnp.where(core == 0, first, second)
        sent[...] = jnp.where(core == 0, second, first)


def moments_part(speed, place, flat, part, from_left, from_right, kind, high, low):
    steps = HALF // CHUNK
    rows = CHUNK * COLUMNS
    lower = pl.BlockSpec((COLUMNS, CHUNK, ROWS), lambda i: (0, i, 0))
    upper = pl.BlockSpec((COLUMNS, CHUNK, ROWS), lambda i: (0, i + steps, 0))
    halo = pl.BlockSpec((3, CHUNK, ROWS), lambda i: (0, i, 0))
    basis_lower = pl.BlockSpec((MOMENTS, CHUNK), lambda i: (0, i))
    basis_upper = pl.BlockSpec((MOMENTS, CHUNK), lambda i: (0, i + steps))
    moved = jax.ShapeDtypeStruct((COLUMNS, HALF, ROWS), F32)
    piece = jax.ShapeDtypeStruct((CELLS // 2, MOMENTS), F32)
    return pl.pallas_call(
        moments_kernel,
        name="faces_and_moments",
        grid=(steps,),
        in_specs=[
            SM,
            SM,
            pl.BlockSpec((rows, ROWS), lambda i: (i, 0)),
            pl.BlockSpec((rows, ROWS), lambda i: (i + steps, 0)),
            lower,
            upper,
            halo,
            halo,
            VM,
            basis_lower,
            basis_lower,
            basis_upper,
            basis_upper,
        ],
        out_specs=[lower, lower, VM, VM],
        out_shape=[moved, moved, piece, piece],
        scratch_shapes=[pltpu.VMEM((MOMENTS, CELLS), F32)],
        compiler_params=params(),
    )(speed, place, flat, flat, part, part, from_left, from_right, kind, high, low, high, low)


def small_call(kernel, name, count, shape, operands, smem=0, scratch=()):
    out = [jax.ShapeDtypeStruct(shape, F32)] * count
    return pl.pallas_call(
        kernel,
        name=name,
        in_specs=[SM] * smem + [VM] * (len(operands) - smem),
        out_specs=[VM] * count if count > 1 else VM,
        out_shape=out if count > 1 else out[0],
        scratch_shapes=scratch,
        compiler_params=params(),
    )(*operands)


def scatter_kernel(place, kept, received, own, to_one, to_two, to_three):
    for away, out in enumerate((own, to_one, to_two, to_three)):
        at = pl.multiple_of(((place[1] + away) % 4) * GROUP, GROUP)
        out[...] = kept[pl.ds(at, GROUP), :] + received[pl.ds(at, GROUP), :]


def add_four_kernel(a, b, c, d, out):
    out[...] = (a[...] + b[...]) + (c[...] + d[...])


def add_two_kernel(a, b, out):
    out[...] = a[...] + b[...]


def collision_kernel(mine, theirs, high, low, out):
    def times(values, which, product):
        top, rest = halves(values)
        both = product(jnp.concatenate([top, rest], axis=0), high[which])
        return both[:GROUP] + (both[GROUP:] + product(top, low[which]))

    moments = mine[...] + theirs[...]
    terms = times(moments, 0, dot_nt) * times(moments, 1, dot_nt)
    out[...] = times(terms, 2, dot)


def relax_kernel(
    place, own, y_1, y_2, y_3, other, z_1, z_2, z_3, kind, moved_lower, moved_upper,
    high, low, out, collision_high, collision_low,
):
    step = pl.program_id(0)

    @pl.when(step == 0)
    def _():
        pieces = (((own, y_1, y_2, y_3), place[0]), ((other, z_1, z_2, z_3), 1 - place[0]))
        for group, core in pieces:
            for away, piece in enumerate(group):
                at = core * 4 + (place[1] + (4 - away)) % 4
                at = pl.multiple_of(at * GROUP, GROUP)
                top, rest = halves(piece[...])
                collision_high[pl.ds(at, GROUP), :] = top
                collision_low[pl.ds(at, GROUP), :] = rest

    top = collision_high[...]
    gain = dot_nt(high[...], top) + (dot_nt(high[...], collision_low[...]) + dot_nt(low[...], top))
    in_upper = step >= HALF // CHUNK
    for x in range(COLUMNS):
        fluid = HALF_STEP * (1 - kind[x : x + 1, :]).astype(F32)
        moved = jnp.where(in_upper, moved_upper[x], moved_lower[x])
        out[pl.ds(x, CHUNK, stride=COLUMNS), :] = (
            moved + fluid * gain[:, x * ROWS : (x + 1) * ROWS]
        )


def relax(place, pieces, kind, moved_lower, moved_upper, high, low):
    steps = PER_DEVICE // CHUNK
    last = steps // 2 - 1
    turned = pl.BlockSpec((CHUNK, MOMENTS), lambda i: (i, 0))
    return pl.pallas_call(
        relax_kernel,
        name="relax",
        grid=(steps,),
        in_specs=[SM]
        + [VM] * 9
        + [
            pl.BlockSpec((COLUMNS, CHUNK, ROWS), lambda i: (0, jnp.minimum(i, last), 0)),
            pl.BlockSpec((COLUMNS, CHUNK, ROWS), lambda i: (0, jnp.maximum(i - last - 1, 0), 0)),
            turned,
            turned,
        ],
        out_specs=pl.BlockSpec((CHUNK * COLUMNS, ROWS), lambda i: (i, 0)),
        out_shape=jax.ShapeDtypeStruct((PER_DEVICE * COLUMNS, ROWS), F32),
        scratch_shapes=[pltpu.VMEM((CELLS, MOMENTS), BF16)] * 2,
        compiler_params=params(),
    )(place, *pieces, kind, moved_lower, moved_upper, high, low)


def on_device(dist, basis, left_factor, right_factor, mixing, next_cell, prev_cell, cell_kind):
    owner = lax.axis_index("vel")
    place = jnp.stack([owner % 2, owner // 4]).astype(jnp.int32)
    speed = ((MIDDLE - owner.astype(F32)) * STEP * RATIO_X).reshape(1)
    flat = dist.reshape(PER_DEVICE * COLUMNS, ROWS)
    to_right, to_left = pack(flat)
    from_left = shifted(to_right, 1)
    from_right = shifted(to_left, -1)

    mine = jnp.concatenate([left_factor, right_factor, mixing.T], axis=0)
    groups = [[4 * y + 2 * z + c for y in range(4) for c in range(2)] for z in range(2)]
    factors = lax.all_gather(mine, "vel", axis=0, tiled=True, axis_index_groups=groups)
    factor_high, factor_low = split_factors(factors.reshape(8, 3, 128, MOMENTS))
    high, low, turned_high, turned_low = split_basis(basis)
    part = local_part(speed, flat, cell_kind, row_tables(next_cell, prev_cell))

    moved_lower, moved_upper, kept, sent = moments_part(
        speed, place, flat, part, from_left, from_right, cell_kind, high, low
    )
    shape = (GROUP, MOMENTS)
    operands = (place, kept, exchanged(sent, 1))
    own, *others = small_call(scatter_kernel, "scatter", 4, shape, operands, 1)
    arrived = [along_y(piece, away + 1) for away, piece in enumerate(others)]
    summed = small_call(add_four_kernel, "add_four", 1, shape, (own, *arrived))
    operands = (summed, exchanged(summed, 2), factor_high, factor_low)
    share = small_call(collision_kernel, "collide", 1, shape, operands)
    whole = small_call(add_two_kernel, "add_two", 1, shape, (share, exchanged(share, 2)))
    pieces = [whole] + [along_y(whole, away) for away in (1, 2, 3)]
    pieces = pieces + [exchanged(piece, 1) for piece in pieces]
    out = relax(place, pieces, cell_kind, moved_lower, moved_upper, turned_high, turned_low)
    return out.reshape(dist.shape)


def solution(mesh):
    in_specs = (
        P("vel", "cells", None),
        P(None, "vel"),
        P("vel", None),
        P("vel", None),
        P(None, "vel"),
        P("cells", None),
        P("cells", None),
        P("cells", None),
    )
    out_specs = P("vel", "cells", None)
    return jax.shard_map(
        on_device, mesh=mesh, in_specs=in_specs, out_specs=out_specs, check_vma=False
    )
```

```python
import functools

import jax
import jax.numpy as jnp
from jax import lax
from jax.experimental import pallas as pl
from jax.experimental.pallas import tpu as pltpu
from jax.sharding import PartitionSpec as P

POINTS = 32
STEP = 6.4 / POINTS
MIDDLE = (POINTS - 1) * 0.5
RATIO_X = 0.2
RATIO_Y = 0.12
HALF_STEP = 0.5

COLUMNS = 4
ROWS = 128
PER_DEVICE = 2048
HALF = PER_DEVICE // 2
CHUNK = 256
MOMENTS = 512
RANKS = 1024
F32 = jnp.float32
BF16 = jnp.bfloat16
MIB = 1 << 20
UP = (0, 1, 2, 3)
DOWN = (3, 2, 1, 0)
EVERY = (0, 1, 2, 3)


def shifted(x, by):
    size = lax.axis_size("cells")
    return lax.ppermute(x, "cells", [(i, (i + by) % size) for i in range(size)])


def exchanged(x, bit):
    return lax.ppermute(x, "vel", [(i, i ^ bit) for i in range(16)])


def along_y(x, by):
    return lax.ppermute(x, "vel", [(i, (i + 4 * by) % 16) for i in range(16)])


def halves(x):
    high = x.astype(BF16)
    return high, (x - high.astype(F32)).astype(BF16)


def minmod(a, b):
    return jnp.maximum(jnp.minimum(a, b), 0.0) + jnp.minimum(jnp.maximum(a, b), 0.0)


def dot(a, b):
    return jnp.dot(a, b, preferred_element_type=F32)


def dot_nt(a, b):
    return lax.dot_general(a, b, (((1,), (1,)), ((), ())), preferred_element_type=F32)


def column(ref, x, count=CHUNK):
    return ref[pl.ds(x, count, stride=COLUMNS), :]


def params(mib):
    return pltpu.CompilerParams(vmem_limit_bytes=mib * MIB)


def cost(flops, size):
    return pl.CostEstimate(flops=flops, bytes_accessed=size, transcendentals=0)


VM = pl.BlockSpec(memory_space=pltpu.VMEM)
SM = pl.BlockSpec(memory_space=pltpu.SMEM)


def pack_kernel(flat, right, left):
    upper = flat.at[pl.ds(HALF * COLUMNS, HALF * COLUMNS)]
    right[0] = column(upper, 3, HALF)
    right[1] = column(upper, 2, HALF)
    right[2] = column(flat, 3, HALF)
    left[0] = column(flat, 0, HALF)
    left[1] = column(flat, 1, HALF)
    left[2] = column(upper, 0, HALF)


def pack(flat):
    out = jax.ShapeDtypeStruct((3, HALF, ROWS), F32)
    return pl.pallas_call(
        pack_kernel,
        name="pack",
        in_specs=[VM],
        out_specs=[VM, VM],
        out_shape=[out, out],
        compiler_params=params(12),
        cost_estimate=cost(1 << 20, 8 * MIB),
    )(flat)


def local_kernel(speed, dist, kind, tables, out):
    step = pl.program_id(0)
    in_upper = step >= HALF // CHUNK
    line = lax.broadcasted_iota(jnp.int32, (CHUNK, ROWS), 0) + step * CHUNK
    along = (line // POINTS) % POINTS
    along = jnp.where(in_upper, POINTS - 1 - along, along)
    courant_y = jnp.abs((along.astype(F32) - MIDDLE) * STEP * RATIO_Y)
    slope_y = 0.5 * (1.0 - courant_y)
    courant_x = speed[0]
    slope_x = 0.5 * (1.0 - courant_x)
    fields = []
    for x in range(COLUMNS):
        here = column(dist, x)
        both = dot(jnp.concatenate(halves(here), axis=1), tables[0, x])
        face = here + slope_y * minmod(here - both[:, :ROWS], both[:, ROWS:] - here)
        behind = dot(jnp.concatenate(halves(face), axis=1), tables[0, x, :, :ROWS])
        fields.append((here, courant_y * (face - behind)))

    def finish(order):
        here = [fields[x][0] for x in order]
        change = [fields[x][1] for x in order]
        fluid = [(1 - kind[x : x + 1, :]).astype(F32) for x in order]
        face_1 = courant_x * (here[1] + slope_x * minmod(here[1] - here[0], here[2] - here[1]))
        face_2 = courant_x * (here[2] + slope_x * minmod(here[2] - here[1], here[3] - here[2]))
        out[order[0]] = here[0] - fluid[0] * change[0]
        out[order[1]] = here[1] - fluid[1] * (change[1] + face_1)
        out[order[2]] = here[2] - fluid[2] * (change[2] + (face_2 - face_1))
        out[order[3]] = here[3] - fluid[3] * (change[3] - face_2)

    @pl.when(in_upper)
    def _():
        finish((0, 1, 2, 3))

    @pl.when(jnp.logical_not(in_upper))
    def _():
        finish((3, 2, 1, 0))


def local_part(speed, flat, kind, tables):
    steps = PER_DEVICE // CHUNK
    quarter = steps // 4

    def against(i):
        return jnp.where((i >= quarter) & (i < 3 * quarter), 0, 1)

    return pl.pallas_call(
        local_kernel,
        name="local_transport",
        grid=(steps,),
        in_specs=[
            SM,
            pl.BlockSpec((CHUNK * COLUMNS, ROWS), lambda i: (i, 0)),
            VM,
            pl.BlockSpec((1, COLUMNS, 2 * ROWS, 2 * ROWS), lambda i: (against(i), 0, 0, 0)),
        ],
        out_specs=pl.BlockSpec((COLUMNS, CHUNK, ROWS), lambda i: (0, i, 0)),
        out_shape=jax.ShapeDtypeStruct((COLUMNS, PER_DEVICE, ROWS), F32),
        compiler_params=params(12),
        cost_estimate=cost(4 << 30, 10 * MIB),
    )(speed, flat, kind, tables)


def row_tables(following, preceding):
    rows = jnp.arange(ROWS, dtype=jnp.int32)[None, :, None]
    after = (rows == following[:, None, :]).astype(BF16)
    before = (rows == preceding[:, None, :]).astype(BF16)
    forward = jnp.concatenate([before, after], axis=2)
    backward = jnp.concatenate([after, before], axis=2)
    forward = jnp.concatenate([forward, forward], axis=1)
    backward = jnp.concatenate([backward, backward], axis=1)
    return jnp.stack([forward, backward])


def basis_kernel(basis, high, low, turned_high, turned_low):
    values = basis[...]
    high[...], low[...] = halves(values)
    turned_high[...], turned_low[...] = halves(values.T)


def split_basis(basis):
    width = 256
    flat = pl.BlockSpec((MOMENTS, width), lambda i: (0, i))
    turned = pl.BlockSpec((width, MOMENTS), lambda i: (i, 0))
    return pl.pallas_call(
        basis_kernel,
        name="split_basis",
        grid=(PER_DEVICE // width,),
        in_specs=[flat],
        out_specs=[flat, flat, turned, turned],
        out_shape=[jax.ShapeDtypeStruct((MOMENTS, PER_DEVICE), BF16)] * 2
        + [jax.ShapeDtypeStruct((PER_DEVICE, MOMENTS), BF16)] * 2,
        compiler_params=params(8),
        cost_estimate=cost(1 << 24, 12 * MIB),
    )(basis)


def stack_kernel(left, right, mixing, out):
    out[:128] = left[...]
    out[128:256] = right[...]
    out[256:] = mixing[...].T


def split_kernel(given, high, low):
    for which in range(3):
        high[which], low[which] = halves(given[which * 128 : (which + 1) * 128])


def gathered_factors(left, right, mixing):
    own = pl.pallas_call(
        stack_kernel,
        name="stack_factors",
        in_specs=[VM] * 3,
        out_specs=VM,
        out_shape=jax.ShapeDtypeStruct((384, MOMENTS), F32),
        compiler_params=params(3),
        cost_estimate=cost(1 << 20, 2 * MIB),
    )(left, right, mixing)
    groups = [[4 * y + 2 * z + c for y in range(4) for c in range(2)] for z in range(2)]
    every = lax.all_gather(own, "vel", axis=0, tiled=True, axis_index_groups=groups)
    out = jax.ShapeDtypeStruct((3, RANKS, MOMENTS), BF16)
    spec = pl.BlockSpec((3, 128, MOMENTS), lambda i: (0, i, 0))
    return pl.pallas_call(
        split_kernel,
        name="split_factors",
        grid=(RANKS // 128,),
        in_specs=[pl.BlockSpec((384, MOMENTS), lambda i: (i, 0))],
        out_specs=[spec, spec],
        out_shape=[out, out],
        compiler_params=params(6),
        cost_estimate=cost(1 << 24, 12 * MIB),
    )(every)


def moments_kernel(
    columns, speed, place, lower, upper, part_lower, part_upper, from_left, from_right, kind,
    high_lower, low_lower, high_upper, low_upper, moved, kept, sent, total,
):
    step = pl.program_id(0)
    courant = speed[0]
    slope = 0.5 * (1.0 - courant)

    def half(dist, part, out, order, behind, behind_two, ahead):
        fluid = [courant * (1 - kind[x : x + 1, :]).astype(F32) for x in order]
        first, second = column(dist, order[0]), column(dist, order[1])
        face_0 = first + slope * minmod(first - behind, second - first)
        values = {order[2]: part[order[2]]}
        values[order[1]] = part[order[1]] + fluid[1] * face_0
        if order[0] in columns:
            third, fourth = column(dist, order[2]), column(dist, order[3])
            face_in = behind + slope * minmod(behind - behind_two, first - behind)
            face_3 = fourth + slope * minmod(fourth - third, ahead - fourth)
            values[order[0]] = part[order[0]] - fluid[0] * (face_0 - face_in)
            values[order[3]] = part[order[3]] - fluid[3] * face_3
        values = [values[x] for x in columns]
        for i, value in enumerate(values):
            moved[out, i] = value
        return halves(jnp.concatenate(values, axis=1))

    @pl.when(step == 0)
    def _():
        total[...] = jnp.zeros_like(total)

    top, rest = half(lower, part_lower, 0, DOWN, from_right[0], from_right[1], from_left[2])
    added = total[...] + dot(high_lower[...], top)
    added = added + dot(high_lower[...], rest)
    added = added + dot(low_lower[...], top)
    top, rest = half(upper, part_upper, 1, UP, from_left[0], from_left[1], from_right[2])
    added = added + dot(high_upper[...], top)
    added = added + dot(high_upper[...], rest)
    added = added + dot(low_upper[...], top)
    total[...] = added

    @pl.when(step == pl.num_programs(0) - 1)
    def _():
        count = total.shape[1] // 2
        core = place[0]
        first = total[:, :count].T
        second = total[:, count:].T
        kept[...] = jnp.where(core == 0, first, second)
        sent[...] = jnp.where(core == 0, second, first)


def moments_part(columns, speed, place, flat, part, from_left, from_right, kind, high, low):
    steps = HALF // CHUNK
    rows = CHUNK * COLUMNS
    count = len(columns)
    lower = pl.BlockSpec((COLUMNS, CHUNK, ROWS), lambda i: (0, i, 0))
    upper = pl.BlockSpec((COLUMNS, CHUNK, ROWS), lambda i: (0, i + steps, 0))
    halo = pl.BlockSpec((3, CHUNK, ROWS), lambda i: (0, i, 0))
    basis_lower = pl.BlockSpec((MOMENTS, CHUNK), lambda i: (0, i))
    basis_upper = pl.BlockSpec((MOMENTS, CHUNK), lambda i: (0, i + steps))
    piece = jax.ShapeDtypeStruct((count * ROWS // 2, MOMENTS), F32)
    return pl.pallas_call(
        functools.partial(moments_kernel, columns),
        name="faces_and_moments",
        grid=(steps,),
        in_specs=[
            SM,
            SM,
            pl.BlockSpec((rows, ROWS), lambda i: (i, 0)),
            pl.BlockSpec((rows, ROWS), lambda i: (i + steps, 0)),
            lower,
            upper,
            halo,
            halo,
            VM,
            basis_lower,
            basis_lower,
            basis_upper,
            basis_upper,
        ],
        out_specs=[pl.BlockSpec((2, count, CHUNK, ROWS), lambda i: (0, 0, i, 0)), VM, VM],
        out_shape=[jax.ShapeDtypeStruct((2, count, HALF, ROWS), F32), piece, piece],
        scratch_shapes=[pltpu.VMEM((MOMENTS, count * ROWS), F32)],
        compiler_params=params(18),
        cost_estimate=cost(8 << 30, 20 * MIB),
    )(speed, place, flat, flat, part, part, from_left, from_right, kind, high, low, high, low)


def small_call(kernel, name, count, shape, operands, smem=0, mib=3):
    out = [jax.ShapeDtypeStruct(shape, F32)] * count
    return pl.pallas_call(
        kernel,
        name=name,
        in_specs=[SM] * smem + [VM] * (len(operands) - smem),
        out_specs=[VM] * count if count > 1 else VM,
        out_shape=out if count > 1 else out[0],
        compiler_params=params(mib),
        cost_estimate=cost(1 << 20, 1 * MIB),
    )(*operands)


def scatter_kernel(place, kept, received, own, to_one, to_two, to_three):
    size = own.shape[0]
    for away, out in enumerate((own, to_one, to_two, to_three)):
        at = pl.multiple_of(((place[1] + away) % 4) * size, size)
        out[...] = kept[pl.ds(at, size), :] + received[pl.ds(at, size), :]


def add_four_kernel(a, b, c, d, out):
    out[...] = (a[...] + b[...]) + (c[...] + d[...])


def add_two_kernel(a, b, out):
    out[...] = a[...] + b[...]


def collision_kernel(mine, theirs, high, low, out):
    size = out.shape[0]

    def times(values, which, product):
        top, rest = halves(values)
        both = product(jnp.concatenate([top, rest], axis=0), high[which])
        return both[:size] + (both[size:] + product(top, low[which]))

    moments = mine[...] + theirs[...]
    terms = times(moments, 0, dot_nt) * times(moments, 1, dot_nt)
    out[...] = times(terms, 2, dot)


def collision_part(place, kept, sent, factor_high, factor_low):
    shape = (kept.shape[0] // 4, MOMENTS)
    operands = (place, kept, exchanged(sent, 1))
    own, *others = small_call(scatter_kernel, "scatter", 4, shape, operands, 1)
    arrived = [along_y(piece, away + 1) for away, piece in enumerate(others)]
    summed = small_call(add_four_kernel, "add_four", 1, shape, (own, *arrived))
    operands = (summed, exchanged(summed, 2), factor_high, factor_low)
    share = small_call(collision_kernel, "collide", 1, shape, operands, mib=10)
    whole = small_call(add_two_kernel, "add_two", 1, shape, (share, exchanged(share, 2)))
    pieces = [whole] + [along_y(whole, away) for away in (1, 2, 3)]
    return pieces + [exchanged(piece, 1) for piece in pieces]


def relax_kernel(
    columns, place, own, y_1, y_2, y_3, other, z_1, z_2, z_3, kind, moved,
    high, low, out, gathered, turned_high, turned_low,
):
    step = pl.program_id(0)
    size = own.shape[0]

    @pl.when(step == 0)
    def _():
        pieces = (((own, y_1, y_2, y_3), place[0]), ((other, z_1, z_2, z_3), 1 - place[0]))
        for group, core in pieces:
            for away, piece in enumerate(group):
                at = core * 4 + (place[1] + (4 - away)) % 4
                gathered[pl.ds(pl.multiple_of(at * size, size), size), :] = piece[...]
        turned_high[...], turned_low[...] = halves(gathered[...].T)

    gain = dot(high[...], turned_high[...])
    gain = gain + dot(high[...], turned_low[...])
    gain = gain + dot(low[...], turned_high[...])
    for i, x in enumerate(columns):
        fluid = HALF_STEP * (1 - kind[x : x + 1, :]).astype(F32)
        out[pl.ds(x, CHUNK, stride=COLUMNS), :] = (
            moved[0, i] + fluid * gain[:, i * ROWS : (i + 1) * ROWS]
        )


def relax(columns, place, pieces, kind, moved, high, low):
    steps = PER_DEVICE // CHUNK
    half = steps // 2
    count = len(columns)
    turned = pl.BlockSpec((CHUNK, MOMENTS), lambda i: (i, 0))
    return pl.pallas_call(
        functools.partial(relax_kernel, columns),
        name="relax",
        grid=(steps,),
        in_specs=[SM]
        + [VM] * 9
        + [
            pl.BlockSpec((1, count, CHUNK, ROWS), lambda i: (i // half, 0, i % half, 0)),
            turned,
            turned,
        ],
        out_specs=pl.BlockSpec((CHUNK * COLUMNS, ROWS), lambda i: (i, 0)),
        out_shape=jax.ShapeDtypeStruct((PER_DEVICE * COLUMNS, ROWS), F32),
        scratch_shapes=[
            pltpu.VMEM((count * ROWS, MOMENTS), F32),
            pltpu.VMEM((MOMENTS, count * ROWS), BF16),
            pltpu.VMEM((MOMENTS, count * ROWS), BF16),
        ],
        compiler_params=params(14),
        cost_estimate=cost(8 << 30, 16 * MIB),
    )(place, *pieces, kind, moved, high, low)


def on_device(dist, basis, left_factor, right_factor, mixing, next_cell, prev_cell, cell_kind):
    owner = lax.axis_index("vel")
    place = jnp.stack([owner % 2, owner // 4]).astype(jnp.int32)
    speed = ((MIDDLE - owner.astype(F32)) * STEP * RATIO_X).reshape(1)
    flat = dist.reshape(PER_DEVICE * COLUMNS, ROWS)
    to_right, to_left = pack(flat)
    from_left = shifted(to_right, 1)
    from_right = shifted(to_left, -1)

    given = (left_factor, right_factor, mixing)
    _, (left_factor, right_factor, mixing) = lax.optimization_barrier((to_left, given))
    factors = gathered_factors(left_factor, right_factor, mixing)
    high, low, turned_high, turned_low = split_basis(basis)
    part = local_part(speed, flat, cell_kind, row_tables(next_cell, prev_cell))
    halo = (from_left, from_right)
    (from_left, from_right), factors = lax.optimization_barrier((halo, factors))

    moved, kept, sent = moments_part(
        EVERY, speed, place, flat, part, from_left, from_right, cell_kind, high, low
    )
    pieces = collision_part(place, kept, sent, *factors)
    out = relax(EVERY, place, pieces, cell_kind, moved, turned_high, turned_low)
    return out.reshape(dist.shape)


def solution(mesh):
    in_specs = (
        P("vel", "cells", None),
        P(None, "vel"),
        P("vel", None),
        P("vel", None),
        P(None, "vel"),
        P("cells", None),
        P("cells", None),
        P("cells", None),
    )
    out_specs = P("vel", "cells", None)
    return jax.shard_map(
        on_device, mesh=mesh, in_specs=in_specs, out_specs=out_specs, check_vma=False
    )
```

```python
import functools

import jax
import jax.numpy as jnp
from jax import lax
from jax.experimental import pallas as pl
from jax.experimental.pallas import tpu as pltpu
from jax.sharding import PartitionSpec as P

POINTS = 32
STEP = 6.4 / POINTS
MIDDLE = (POINTS - 1) * 0.5
RATIO_X = 0.2
RATIO_Y = 0.12
HALF_STEP = 0.5

COLUMNS = 4
ROWS = 128
PER_DEVICE = 2048
HALF = PER_DEVICE // 2
CHUNK = 256
MOMENTS = 512
RANKS = 1024
F32 = jnp.float32
BF16 = jnp.bfloat16
MIB = 1 << 20
UP = (0, 1, 2, 3)
DOWN = (3, 2, 1, 0)
INNER = (1, 2)
OUTER = (0, 3)


def shifted(x, by):
    size = lax.axis_size("cells")
    return lax.ppermute(x, "cells", [(i, (i + by) % size) for i in range(size)])


def exchanged(x, bit):
    return lax.ppermute(x, "vel", [(i, i ^ bit) for i in range(16)])


def along_y(x, by):
    return lax.ppermute(x, "vel", [(i, (i + 4 * by) % 16) for i in range(16)])


def halves(x):
    high = x.astype(BF16)
    return high, (x - high.astype(F32)).astype(BF16)


def minmod(a, b):
    return jnp.maximum(jnp.minimum(a, b), 0.0) + jnp.minimum(jnp.maximum(a, b), 0.0)


def dot(a, b):
    return jnp.dot(a, b, preferred_element_type=F32)


def dot_nt(a, b):
    return lax.dot_general(a, b, (((1,), (1,)), ((), ())), preferred_element_type=F32)


def column(ref, x, count=CHUNK):
    return ref[pl.ds(x, count, stride=COLUMNS), :]


def params(mib):
    return pltpu.CompilerParams(vmem_limit_bytes=mib * MIB)


def cost(flops, size):
    return pl.CostEstimate(flops=flops, bytes_accessed=size, transcendentals=0)


VM = pl.BlockSpec(memory_space=pltpu.VMEM)
SM = pl.BlockSpec(memory_space=pltpu.SMEM)


def pack_kernel(flat, right_near, left_near, right_far, left_far):
    upper = flat.at[pl.ds(HALF * COLUMNS, HALF * COLUMNS)]
    right_near[...] = column(upper, 3, HALF)
    left_near[...] = column(flat, 0, HALF)
    right_far[0] = column(upper, 2, HALF)
    right_far[1] = column(flat, 3, HALF)
    left_far[0] = column(flat, 1, HALF)
    left_far[1] = column(upper, 0, HALF)


def pack(flat):
    near = jax.ShapeDtypeStruct((HALF, ROWS), F32)
    far = jax.ShapeDtypeStruct((2, HALF, ROWS), F32)
    return pl.pallas_call(
        pack_kernel,
        name="pack",
        in_specs=[VM],
        out_specs=[VM] * 4,
        out_shape=[near, near, far, far],
        compiler_params=params(12),
        cost_estimate=cost(1 << 20, 8 * MIB),
    )(flat)


def staged(stage, operands):
    shapes = jax.eval_shape(stage, *operands)
    blank = lambda *_: jax.tree.map(lambda x: jnp.zeros(x.shape, x.dtype), shapes)
    taken = lax.optimization_barrier(jnp.array(True))
    return lax.cond(taken, stage, blank, *operands)


def local_kernel(speed, dist, kind, tables, out):
    step = pl.program_id(0)
    in_upper = step >= HALF // CHUNK
    line = lax.broadcasted_iota(jnp.int32, (CHUNK, ROWS), 0) + step * CHUNK
    along = (line // POINTS) % POINTS
    along = jnp.where(in_upper, POINTS - 1 - along, along)
    courant_y = jnp.abs((along.astype(F32) - MIDDLE) * STEP * RATIO_Y)
    slope_y = 0.5 * (1.0 - courant_y)
    courant_x = speed[0]
    slope_x = 0.5 * (1.0 - courant_x)
    fields = []
    for x in range(COLUMNS):
        here = column(dist, x)
        both = dot(jnp.concatenate(halves(here), axis=1), tables[0, x])
        face = here + slope_y * minmod(here - both[:, :ROWS], both[:, ROWS:] - here)
        behind = dot(jnp.concatenate(halves(face), axis=1), tables[0, x, :, :ROWS])
        fields.append((here, courant_y * (face - behind)))

    def finish(order):
        here = [fields[x][0] for x in order]
        change = [fields[x][1] for x in order]
        fluid = [(1 - kind[x : x + 1, :]).astype(F32) for x in order]
        face_1 = courant_x * (here[1] + slope_x * minmod(here[1] - here[0], here[2] - here[1]))
        face_2 = courant_x * (here[2] + slope_x * minmod(here[2] - here[1], here[3] - here[2]))
        out[order[0]] = here[0] - fluid[0] * change[0]
        out[order[1]] = here[1] - fluid[1] * (change[1] + face_1)
        out[order[2]] = here[2] - fluid[2] * (change[2] + (face_2 - face_1))
        out[order[3]] = here[3] - fluid[3] * (change[3] - face_2)

    @pl.when(in_upper)
    def _():
        finish((0, 1, 2, 3))

    @pl.when(jnp.logical_not(in_upper))
    def _():
        finish((3, 2, 1, 0))


def local_part(speed, flat, kind, tables):
    steps = PER_DEVICE // CHUNK
    quarter = steps // 4

    def against(i):
        return jnp.where((i >= quarter) & (i < 3 * quarter), 0, 1)

    return pl.pallas_call(
        local_kernel,
        name="local_transport",
        grid=(steps,),
        in_specs=[
            SM,
            pl.BlockSpec((CHUNK * COLUMNS, ROWS), lambda i: (i, 0)),
            VM,
            pl.BlockSpec((1, COLUMNS, 2 * ROWS, 2 * ROWS), lambda i: (against(i), 0, 0, 0)),
        ],
        out_specs=pl.BlockSpec((COLUMNS, CHUNK, ROWS), lambda i: (0, i, 0)),
        out_shape=jax.ShapeDtypeStruct((COLUMNS, PER_DEVICE, ROWS), F32),
        compiler_params=params(12),
        cost_estimate=cost(4 << 30, 10 * MIB),
    )(speed, flat, kind, tables)


def row_tables(following, preceding):
    rows = jnp.arange(ROWS, dtype=jnp.int32)[None, :, None]
    after = (rows == following[:, None, :]).astype(BF16)
    before = (rows == preceding[:, None, :]).astype(BF16)
    forward = jnp.concatenate([before, after], axis=2)
    backward = jnp.concatenate([after, before], axis=2)
    forward = jnp.concatenate([forward, forward], axis=1)
    backward = jnp.concatenate([backward, backward], axis=1)
    return jnp.stack([forward, backward])


def basis_kernel(basis, high, low, turned_high, turned_low):
    values = basis[...]
    high[...], low[...] = halves(values)
    turned_high[...], turned_low[...] = halves(values.T)


def split_basis(basis):
    width = 256
    flat = pl.BlockSpec((MOMENTS, width), lambda i: (0, i))
    turned = pl.BlockSpec((width, MOMENTS), lambda i: (i, 0))
    return pl.pallas_call(
        basis_kernel,
        name="split_basis",
        grid=(PER_DEVICE // width,),
        in_specs=[flat],
        out_specs=[flat, flat, turned, turned],
        out_shape=[jax.ShapeDtypeStruct((MOMENTS, PER_DEVICE), BF16)] * 2
        + [jax.ShapeDtypeStruct((PER_DEVICE, MOMENTS), BF16)] * 2,
        compiler_params=params(8),
        cost_estimate=cost(1 << 24, 12 * MIB),
    )(basis)


def stack_kernel(left, right, mixing, out):
    out[:128] = left[...]
    out[128:256] = right[...]
    out[256:] = mixing[...].T


def split_kernel(given, high, low):
    for which in range(3):
        high[which], low[which] = halves(given[which * 128 : (which + 1) * 128])


def gathered_factors(left, right, mixing):
    own = pl.pallas_call(
        stack_kernel,
        name="stack_factors",
        in_specs=[VM] * 3,
        out_specs=VM,
        out_shape=jax.ShapeDtypeStruct((384, MOMENTS), F32),
        compiler_params=params(3),
        cost_estimate=cost(1 << 20, 2 * MIB),
    )(left, right, mixing)
    groups = [[4 * y + 2 * z + c for y in range(4) for c in range(2)] for z in range(2)]
    return lax.all_gather(own, "vel", axis=0, tiled=True, axis_index_groups=groups)


def split_factors(factors):
    out = jax.ShapeDtypeStruct((3, RANKS, MOMENTS), BF16)
    spec = pl.BlockSpec((3, 128, MOMENTS), lambda i: (0, i, 0))
    return pl.pallas_call(
        split_kernel,
        name="split_factors",
        grid=(RANKS // 128,),
        in_specs=[pl.BlockSpec((384, MOMENTS), lambda i: (i, 0))],
        out_specs=[spec, spec],
        out_shape=[out, out],
        compiler_params=params(6),
        cost_estimate=cost(1 << 24, 12 * MIB),
    )(factors)


def moments_kernel(
    columns, speed, place, lower, upper, part_lower, part_upper, kind,
    high_lower, low_lower, high_upper, low_upper, left_near, right_near, *rest,
):
    *far, moved, kept, sent, total = rest
    step = pl.program_id(0)
    courant = speed[0]
    slope = 0.5 * (1.0 - courant)

    def half(dist, part, out, order, behind, outer):
        fluid = [courant * (1 - kind[x : x + 1, :]).astype(F32) for x in order]
        first, second = column(dist, order[0]), column(dist, order[1])
        face_0 = first + slope * minmod(first - behind, second - first)
        if outer:
            behind_two, ahead = outer
            third, fourth = column(dist, order[2]), column(dist, order[3])
            face_in = behind + slope * minmod(behind - behind_two, first - behind)
            face_3 = fourth + slope * minmod(fourth - third, ahead - fourth)
            values = {
                order[0]: part[order[0]] - fluid[0] * (face_0 - face_in),
                order[3]: part[order[3]] - fluid[3] * face_3,
            }
        else:
            values = {order[1]: part[order[1]] + fluid[1] * face_0, order[2]: part[order[2]]}
        values = [values[x] for x in columns]
        for i, value in enumerate(values):
            moved[out, i] = value
        return halves(jnp.concatenate(values, axis=1))

    @pl.when(step == 0)
    def _():
        total[...] = jnp.zeros_like(total)

    outer = ((), ())
    if far:
        outer = ((far[1][0], far[0][1]), (far[0][0], far[1][1]))
    top, rest = half(lower, part_lower, 0, DOWN, right_near[...], outer[0])
    added = total[...] + dot(high_lower[...], top)
    added = added + dot(high_lower[...], rest)
    added = added + dot(low_lower[...], top)
    top, rest = half(upper, part_upper, 1, UP, left_near[...], outer[1])
    added = added + dot(high_upper[...], top)
    added = added + dot(high_upper[...], rest)
    added = added + dot(low_upper[...], top)
    total[...] = added

    @pl.when(step == pl.num_programs(0) - 1)
    def _():
        count = total.shape[1] // 2
        core = place[0]
        first = total[:, :count].T
        second = total[:, count:].T
        kept[...] = jnp.where(core == 0, first, second)
        sent[...] = jnp.where(core == 0, second, first)


def moments_part(columns, speed, place, flat, part, kind, high, low, near, far=()):
    steps = HALF // CHUNK
    rows = CHUNK * COLUMNS
    count = len(columns)
    lower = pl.BlockSpec((COLUMNS, CHUNK, ROWS), lambda i: (0, i, 0))
    upper = pl.BlockSpec((COLUMNS, CHUNK, ROWS), lambda i: (0, i + steps, 0))
    basis_lower = pl.BlockSpec((MOMENTS, CHUNK), lambda i: (0, i))
    basis_upper = pl.BlockSpec((MOMENTS, CHUNK), lambda i: (0, i + steps))
    piece = jax.ShapeDtypeStruct((count * ROWS // 2, MOMENTS), F32)
    return pl.pallas_call(
        functools.partial(moments_kernel, columns),
        name="faces_and_moments",
        grid=(steps,),
        in_specs=[
            SM,
            SM,
            pl.BlockSpec((rows, ROWS), lambda i: (i, 0)),
            pl.BlockSpec((rows, ROWS), lambda i: (i + steps, 0)),
            lower,
            upper,
            VM,
            basis_lower,
            basis_lower,
            basis_upper,
            basis_upper,
        ]
        + [pl.BlockSpec((CHUNK, ROWS), lambda i: (i, 0))] * 2
        + [pl.BlockSpec((2, CHUNK, ROWS), lambda i: (0, i, 0))] * len(far),
        out_specs=[pl.BlockSpec((2, count, CHUNK, ROWS), lambda i: (0, 0, i, 0)), VM, VM],
        out_shape=[jax.ShapeDtypeStruct((2, count, HALF, ROWS), F32), piece, piece],
        scratch_shapes=[pltpu.VMEM((MOMENTS, count * ROWS), F32)],
        compiler_params=params(16),
        cost_estimate=cost(8 << 30, 20 * MIB),
    )(speed, place, flat, flat, part, part, kind, high, low, high, low, *near, *far)


def small_call(kernel, name, count, shape, operands, smem=0, mib=3):
    out = [jax.ShapeDtypeStruct(shape, F32)] * count
    return pl.pallas_call(
        kernel,
        name=name,
        in_specs=[SM] * smem + [VM] * (len(operands) - smem),
        out_specs=[VM] * count if count > 1 else VM,
        out_shape=out if count > 1 else out[0],
        compiler_params=params(mib),
        cost_estimate=cost(1 << 20, 1 * MIB),
    )(*operands)


def scatter_kernel(place, kept, received, own, to_one, to_two, to_three):
    size = own.shape[0]
    for away, out in enumerate((own, to_one, to_two, to_three)):
        at = pl.multiple_of(((place[1] + away) % 4) * size, size)
        out[...] = kept[pl.ds(at, size), :] + received[pl.ds(at, size), :]


def add_four_kernel(a, b, c, d, out):
    out[...] = (a[...] + b[...]) + (c[...] + d[...])


def add_two_kernel(a, b, out):
    out[...] = a[...] + b[...]


def collision_kernel(mine, theirs, high, low, out):
    size = out.shape[0]

    def times(values, which, product):
        top, rest = halves(values)
        both = product(jnp.concatenate([top, rest], axis=0), high[which])
        return both[:size] + (both[size:] + product(top, low[which]))

    moments = mine[...] + theirs[...]
    terms = times(moments, 0, dot_nt) * times(moments, 1, dot_nt)
    out[...] = times(terms, 2, dot)


def in_turn(sends, at_once):
    done = []
    for i, (send, piece, *rest) in enumerate(sends):
        if i >= at_once:
            piece, done[i - at_once] = lax.optimization_barrier((piece, done[i - at_once]))
        done.append(send(piece, *rest))
    return done


def summed_moments(place, kept, sent, at_once):
    shape = (kept.shape[0] // 4, MOMENTS)
    operands = (place, kept, exchanged(sent, 1))
    own, *others = small_call(scatter_kernel, "scatter", 4, shape, operands, 1)
    arrived = in_turn([(along_y, piece, i + 1) for i, piece in enumerate(others)], at_once)
    summed = small_call(add_four_kernel, "add_four", 1, shape, (own, *arrived))
    return summed, exchanged(summed, 2)


def collision_part(moments, factor_high, factor_low, at_once):
    shape = moments[0].shape
    operands = (*moments, factor_high, factor_low)
    share = small_call(collision_kernel, "collide", 1, shape, operands, mib=10)
    whole = small_call(add_two_kernel, "add_two", 1, shape, (share, exchanged(share, 2)))
    pieces = [whole] + in_turn([(along_y, whole, away) for away in (1, 2, 3)], at_once)
    return pieces + in_turn([(exchanged, piece, 1) for piece in pieces], at_once)


def relax_kernel(
    columns, place, own, y_1, y_2, y_3, other, z_1, z_2, z_3, kind, moved, high, low, *rest
):
    *finished, out, gathered, turned_high, turned_low = rest
    step = pl.program_id(0)
    size = own.shape[0]

    @pl.when(step == 0)
    def _():
        pieces = (((own, y_1, y_2, y_3), place[0]), ((other, z_1, z_2, z_3), 1 - place[0]))
        for group, core in pieces:
            for away, piece in enumerate(group):
                at = core * 4 + (place[1] + (4 - away)) % 4
                gathered[pl.ds(pl.multiple_of(at * size, size), size), :] = piece[...]
        turned_high[...], turned_low[...] = halves(gathered[...].T)

    gain = dot(high[...], turned_high[...])
    gain = gain + dot(high[...], turned_low[...])
    gain = gain + dot(low[...], turned_high[...])
    for i, x in enumerate(columns):
        fluid = HALF_STEP * (1 - kind[x : x + 1, :]).astype(F32)
        value = moved[0, i] + fluid * gain[:, i * ROWS : (i + 1) * ROWS]
        if finished:
            out[pl.ds(x, CHUNK, stride=COLUMNS), :] = value
            there = INNER[i]
            out[pl.ds(there, CHUNK, stride=COLUMNS), :] = finished[0][0, i]
        else:
            out[0, i] = value


def relax(columns, place, pieces, kind, moved, high, low, finished=()):
    steps = PER_DEVICE // CHUNK
    half = steps // 2
    count = len(columns)
    turned = pl.BlockSpec((CHUNK, MOMENTS), lambda i: (i, 0))
    planes = pl.BlockSpec((1, count, CHUNK, ROWS), lambda i: (i // half, 0, i % half, 0))
    whole = pl.BlockSpec((CHUNK * COLUMNS, ROWS), lambda i: (i, 0))
    shape = (PER_DEVICE * COLUMNS, ROWS) if finished else moved.shape
    return pl.pallas_call(
        functools.partial(relax_kernel, columns),
        name="relax",
        grid=(steps,),
        in_specs=[SM] + [VM] * 9 + [planes, turned, turned] + [planes] * len(finished),
        out_specs=whole if finished else planes,
        out_shape=jax.ShapeDtypeStruct(shape, F32),
        scratch_shapes=[
            pltpu.VMEM((count * ROWS, MOMENTS), F32),
            pltpu.VMEM((MOMENTS, count * ROWS), BF16),
            pltpu.VMEM((MOMENTS, count * ROWS), BF16),
        ],
        compiler_params=params(14),
        cost_estimate=cost(16 << 30, 1 * MIB),
    )(place, *pieces, kind, moved, high, low, *finished)


def on_device(dist, basis, left_factor, right_factor, mixing, next_cell, prev_cell, cell_kind):
    owner = lax.axis_index("vel")
    place = jnp.stack([owner % 2, owner // 4]).astype(jnp.int32)
    speed = ((MIDDLE - owner.astype(F32)) * STEP * RATIO_X).reshape(1)
    flat = dist.reshape(PER_DEVICE * COLUMNS, ROWS)
    right_near, left_near, right_far, left_far = pack(flat)
    near = (shifted(right_near, 1), shifted(left_near, -1))
    far = (shifted(right_far, 1), shifted(left_far, -1))
    given = (left_factor, right_factor, mixing)
    _, given = lax.optimization_barrier((left_near, given))
    factors = gathered_factors(*given)

    def prepare(_, basis, speed, flat, kind, following, preceding):
        part = local_part(speed, flat, kind, row_tables(following, preceding))
        return split_basis(basis), part

    given = (left_near[:8], basis, speed, flat, cell_kind, next_cell, prev_cell)
    bases, part = staged(prepare, given)
    high, low, turned_high, turned_low = bases

    def inner_moments(speed, place, flat, part, kind, high, low, near):
        moved, *pieces = moments_part(
            INNER, speed, place, flat, part, kind, high, low, near
        )
        return moved, summed_moments(place, *pieces, 1)

    given = (speed, place, flat, part, cell_kind, high, low, near)
    moved, moments = staged(inner_moments, given)
    moments, factors = lax.optimization_barrier((moments, factors))

    def inner_collision(moments, factors):
        factors = split_factors(factors)
        pieces = collision_part(moments, *factors, 1)
        return pieces, factors

    pieces, factors = staged(inner_collision, (moments, factors))
    finished = relax(INNER, place, pieces, cell_kind, moved, turned_high, turned_low)
    finished, far = lax.optimization_barrier((finished, far))

    moved, *pieces = moments_part(
        OUTER, speed, place, flat, part, cell_kind, high, low, near, far
    )
    pieces = collision_part(summed_moments(place, *pieces, 4), *factors, 4)
    out = relax(
        OUTER, place, pieces, cell_kind, moved, turned_high, turned_low, (finished,)
    )
    return out.reshape(dist.shape)


def solution(mesh):
    in_specs = (
        P("vel", "cells", None),
        P(None, "vel"),
        P("vel", None),
        P("vel", None),
        P(None, "vel"),
        P("cells", None),
        P("cells", None),
        P("cells", None),
    )
    out_specs = P("vel", "cells", None)
    return jax.shard_map(
        on_device, mesh=mesh, in_specs=in_specs, out_specs=out_specs, check_vma=False
    )
```

```python
import functools

import jax
import jax.numpy as jnp
from jax import lax
from jax.experimental import pallas as pl
from jax.experimental.pallas import tpu as pltpu
from jax.sharding import PartitionSpec as P

POINTS = 32
STEP = 6.4 / POINTS
MIDDLE = (POINTS - 1) * 0.5
RATIO_X = 0.2
RATIO_Y = 0.12
HALF_STEP = 0.5

COLUMNS = 4
ROWS = 128
PER_DEVICE = 2048
HALF = PER_DEVICE // 2
CHUNK = 256
MOMENTS = 512
RANKS = 1024
F32 = jnp.float32
BF16 = jnp.bfloat16
MIB = 1 << 20
UP = (0, 1, 2, 3)
DOWN = (3, 2, 1, 0)
CELLS = COLUMNS * ROWS


def shifted(x, by):
    size = lax.axis_size("cells")
    return lax.ppermute(x, "cells", [(i, (i + by) % size) for i in range(size)])


def exchanged(x, bit):
    return lax.ppermute(x, "vel", [(i, i ^ bit) for i in range(16)])


def along_y(x, by):
    return lax.ppermute(x, "vel", [(i, (i + 4 * by) % 16) for i in range(16)])


def halves(x):
    high = x.astype(BF16)
    return high, (x - high.astype(F32)).astype(BF16)


def minmod(a, b):
    return jnp.maximum(jnp.minimum(a, b), 0.0) + jnp.minimum(jnp.maximum(a, b), 0.0)


def dot(a, b):
    return jnp.dot(a, b, preferred_element_type=F32)


def dot_nt(a, b):
    return lax.dot_general(a, b, (((1,), (1,)), ((), ())), preferred_element_type=F32)


def column(ref, x, count=CHUNK):
    return ref[pl.ds(x, count, stride=COLUMNS), :]


def params(mib):
    return pltpu.CompilerParams(vmem_limit_bytes=mib * MIB)


def cost(flops, size):
    return pl.CostEstimate(flops=flops, bytes_accessed=size, transcendentals=0)


VM = pl.BlockSpec(memory_space=pltpu.VMEM)
SM = pl.BlockSpec(memory_space=pltpu.SMEM)
ANY = pl.BlockSpec(memory_space=pl.ANY)


def pack_kernel(flat, right, left, held, right_held, left_held, arrivals, leavings):
    steps = HALF // CHUNK
    rows = CHUNK * COLUMNS
    copies = []
    for i in range(steps):
        for half in range(2):
            at = pl.ds((half * steps + i) * rows, rows)
            copies.append(
                pltpu.make_async_copy(flat.at[at], held.at[at], arrivals.at[2 * i + half])
            )
    for copy in copies:
        copy.start()
    sends = []
    for i in range(steps):
        lower = held.at[pl.ds(i * rows, rows)]
        upper = held.at[pl.ds((steps + i) * rows, rows)]
        out = pl.ds(i * CHUNK, CHUNK)
        copies[2 * i].wait()
        right_held[2, out, :] = column(lower, 3)
        left_held[0, out, :] = column(lower, 0)
        left_held[1, out, :] = column(lower, 1)
        copies[2 * i + 1].wait()
        right_held[0, out, :] = column(upper, 3)
        right_held[1, out, :] = column(upper, 2)
        left_held[2, out, :] = column(upper, 0)
        for j, (source, target) in enumerate(((right_held, right), (left_held, left))):
            send = pltpu.make_async_copy(
                source.at[:, out], target.at[:, out], leavings.at[2 * i + j]
            )
            send.start()
            sends.append(send)
    for send in sends:
        send.wait()


def pack(flat):
    out = jax.ShapeDtypeStruct((3, HALF, ROWS), F32)
    return pl.pallas_call(
        pack_kernel,
        name="pack",
        in_specs=[ANY],
        out_specs=[ANY, ANY],
        out_shape=[out, out],
        scratch_shapes=[
            pltpu.VMEM((PER_DEVICE * COLUMNS, ROWS), F32),
            pltpu.VMEM((3, HALF, ROWS), F32),
            pltpu.VMEM((3, HALF, ROWS), F32),
            pltpu.SemaphoreType.DMA((2 * HALF // CHUNK,)),
            pltpu.SemaphoreType.DMA((2 * HALF // CHUNK,)),
        ],
        compiler_params=params(58),
        cost_estimate=cost(1 << 20, 8 * MIB),
    )(flat)


def staged(stage, operands):
    shapes = jax.eval_shape(stage, *operands)
    blank = lambda *_: jax.tree.map(lambda x: jnp.zeros(x.shape, x.dtype), shapes)
    taken = lax.optimization_barrier(jnp.array(True))
    return lax.cond(taken, stage, blank, *operands)


def local_kernel(speed, dist, kind, tables, out):
    step = pl.program_id(0)
    in_upper = step >= HALF // CHUNK
    line = lax.broadcasted_iota(jnp.int32, (CHUNK, ROWS), 0) + step * CHUNK
    along = (line // POINTS) % POINTS
    along = jnp.where(in_upper, POINTS - 1 - along, along)
    courant_y = jnp.abs((along.astype(F32) - MIDDLE) * STEP * RATIO_Y)
    slope_y = 0.5 * (1.0 - courant_y)
    courant_x = speed[0]
    slope_x = 0.5 * (1.0 - courant_x)
    fields = []
    for x in range(COLUMNS):
        here = column(dist, x)
        both = dot(jnp.concatenate(halves(here), axis=1), tables[0, x])
        face = here + slope_y * minmod(here - both[:, :ROWS], both[:, ROWS:] - here)
        behind = dot(jnp.concatenate(halves(face), axis=1), tables[0, x, :, :ROWS])
        fields.append((here, courant_y * (face - behind)))

    def finish(order):
        here = [fields[x][0] for x in order]
        change = [fields[x][1] for x in order]
        fluid = [(1 - kind[x : x + 1, :]).astype(F32) for x in order]
        face_1 = courant_x * (here[1] + slope_x * minmod(here[1] - here[0], here[2] - here[1]))
        face_2 = courant_x * (here[2] + slope_x * minmod(here[2] - here[1], here[3] - here[2]))
        out[order[0]] = here[0] - fluid[0] * change[0]
        out[order[1]] = here[1] - fluid[1] * (change[1] + face_1)
        out[order[2]] = here[2] - fluid[2] * (change[2] + (face_2 - face_1))
        out[order[3]] = here[3] - fluid[3] * (change[3] - face_2)

    @pl.when(in_upper)
    def _():
        finish((0, 1, 2, 3))

    @pl.when(jnp.logical_not(in_upper))
    def _():
        finish((3, 2, 1, 0))


def local_part(speed, flat, kind, tables):
    steps = PER_DEVICE // CHUNK
    quarter = steps // 4

    def against(i):
        return jnp.where((i >= quarter) & (i < 3 * quarter), 0, 1)

    return pl.pallas_call(
        local_kernel,
        name="local_transport",
        grid=(steps,),
        in_specs=[
            SM,
            pl.BlockSpec((CHUNK * COLUMNS, ROWS), lambda i: (i, 0)),
            VM,
            pl.BlockSpec((1, COLUMNS, 2 * ROWS, 2 * ROWS), lambda i: (against(i), 0, 0, 0)),
        ],
        out_specs=pl.BlockSpec((COLUMNS, CHUNK, ROWS), lambda i: (0, i, 0)),
        out_shape=jax.ShapeDtypeStruct((COLUMNS, PER_DEVICE, ROWS), F32),
        compiler_params=params(12),
        cost_estimate=cost(4 << 30, 10 * MIB),
    )(speed, flat, kind, tables)


def row_tables(following, preceding):
    rows = jnp.arange(ROWS, dtype=jnp.int32)[None, :, None]
    after = (rows == following[:, None, :]).astype(BF16)
    before = (rows == preceding[:, None, :]).astype(BF16)
    forward = jnp.concatenate([before, after], axis=2)
    backward = jnp.concatenate([after, before], axis=2)
    forward = jnp.concatenate([forward, forward], axis=1)
    backward = jnp.concatenate([backward, backward], axis=1)
    return jnp.stack([forward, backward])


def basis_kernel(basis, high, low, turned_high, turned_low):
    values = basis[...]
    high[...], low[...] = halves(values)
    turned_high[...], turned_low[...] = halves(values.T)


def split_basis(basis):
    width = 256
    flat = pl.BlockSpec((MOMENTS, width), lambda i: (0, i))
    turned = pl.BlockSpec((width, MOMENTS), lambda i: (i, 0))
    return pl.pallas_call(
        basis_kernel,
        name="split_basis",
        grid=(PER_DEVICE // width,),
        in_specs=[flat],
        out_specs=[flat, flat, turned, turned],
        out_shape=[jax.ShapeDtypeStruct((MOMENTS, PER_DEVICE), BF16)] * 2
        + [jax.ShapeDtypeStruct((PER_DEVICE, MOMENTS), BF16)] * 2,
        compiler_params=params(8),
        cost_estimate=cost(1 << 24, 12 * MIB),
    )(basis)


def stack_kernel(left, right, mixing, out):
    out[:128] = left[...]
    out[128:256] = right[...]
    out[256:] = mixing[...].T


def join_kernel(own, before, after, across_top, across_rest, out):
    out[0] = own[...]
    out[1] = before[...]
    out[2] = after[...]
    out[3, :192] = across_top[...]
    out[3, 192:] = across_rest[...]


def split_kernel(mine, theirs, high, low):
    for i, source in enumerate((mine, theirs)):
        for j in range(4):
            rows = pl.ds((4 * i + j) * 128, 128)
            for which in range(3):
                top, rest = halves(source[j, which * 128 : (which + 1) * 128])
                high[which, rows, :] = top
                low[which, rows, :] = rest


def gathered_factors(_, left, right, mixing):
    own = pl.pallas_call(
        stack_kernel,
        name="stack_factors",
        in_specs=[VM] * 3,
        out_specs=VM,
        out_shape=jax.ShapeDtypeStruct((384, MOMENTS), F32),
        compiler_params=params(3),
        cost_estimate=cost(1 << 20, 2 * MIB),
    )(left, right, mixing)
    before, after = along_y(own, 1), along_y(own, -1)
    across_top, across_rest = along_y(before[:192], 1), along_y(after[192:], -1)
    mine = pl.pallas_call(
        join_kernel,
        name="join_factors",
        in_specs=[VM] * 5,
        out_specs=VM,
        out_shape=jax.ShapeDtypeStruct((4, 384, MOMENTS), F32),
        compiler_params=params(8),
        cost_estimate=cost(1 << 20, 6 * MIB),
    )(own, before, after, across_top, across_rest)
    return mine, exchanged(mine, 1)


def split_factors(mine, theirs):
    out = jax.ShapeDtypeStruct((3, RANKS, MOMENTS), BF16)
    return pl.pallas_call(
        split_kernel,
        name="split_factors",
        in_specs=[VM] * 2,
        out_specs=[VM] * 2,
        out_shape=[out, out],
        compiler_params=params(16),
        cost_estimate=cost(1 << 24, 12 * MIB),
    )(mine, theirs)


def moments_kernel(
    speed, place, dist, part, from_left, from_right, kind, high, low, moved, kept, sent, total
):
    step = pl.program_id(0)
    courant = speed[0]
    slope = 0.5 * (1.0 - courant)
    across = pl.ds(pl.multiple_of(step * CHUNK, CHUNK), CHUNK)

    def half(which, order, behind, behind_two, ahead):
        first_line = pl.multiple_of(which * HALF + step * CHUNK, CHUNK)
        lines = pl.ds(first_line, CHUNK)
        fluid = [courant * (1 - kind[x : x + 1, :]).astype(F32) for x in order]
        first, second, third, fourth = (
            dist[pl.ds(first_line * COLUMNS + x, CHUNK, stride=COLUMNS), :] for x in order
        )
        face_in = behind + slope * minmod(behind - behind_two, first - behind)
        face_0 = first + slope * minmod(first - behind, second - first)
        face_3 = fourth + slope * minmod(fourth - third, ahead - fourth)
        values = {
            order[0]: part[order[0], lines, :] - fluid[0] * (face_0 - face_in),
            order[1]: part[order[1], lines, :] + fluid[1] * face_0,
            order[2]: part[order[2], lines, :],
            order[3]: part[order[3], lines, :] - fluid[3] * face_3,
        }
        for x in range(COLUMNS):
            moved[x, lines, :] = values[x]
        return halves(jnp.concatenate([values[x] for x in range(COLUMNS)], axis=1))

    @pl.when(step == 0)
    def _():
        total[...] = jnp.zeros_like(total)

    left, right = from_left, from_right
    added = total[...]
    ends = (
        (DOWN, right[0, across, :], right[1, across, :], left[2, across, :]),
        (UP, left[0, across, :], left[1, across, :], right[2, across, :]),
    )
    for which, end in enumerate(ends):
        top, rest = half(which, *end)
        lines = pl.ds(pl.multiple_of(which * HALF + step * CHUNK, CHUNK), CHUNK)
        added = added + dot(high[:, lines], top)
        added = added + dot(high[:, lines], rest)
        added = added + dot(low[:, lines], top)
    total[...] = added

    @pl.when(step == pl.num_programs(0) - 1)
    def _():
        count = CELLS // 2
        core = place[0]
        first = total[:, :count].T
        second = total[:, count:].T
        kept[...] = jnp.where(core == 0, first, second)
        sent[...] = jnp.where(core == 0, second, first)


def moments_part(speed, place, flat, part, from_left, from_right, kind, high, low):
    piece = jax.ShapeDtypeStruct((CELLS // 2, MOMENTS), F32)
    return pl.pallas_call(
        moments_kernel,
        name="faces_and_moments",
        grid=(HALF // CHUNK,),
        in_specs=[SM, SM] + [VM] * 7,
        out_specs=[VM] * 3,
        out_shape=[jax.ShapeDtypeStruct((COLUMNS, PER_DEVICE, ROWS), F32), piece, piece],
        scratch_shapes=[pltpu.VMEM((MOMENTS, CELLS), F32)],
        compiler_params=params(26),
        cost_estimate=cost(8 << 30, 20 * MIB),
    )(speed, place, flat, part, from_left, from_right, kind, high, low)


def small_call(kernel, name, count, shape, operands, smem=0, mib=3):
    out = [jax.ShapeDtypeStruct(shape, F32)] * count
    return pl.pallas_call(
        kernel,
        name=name,
        in_specs=[SM] * smem + [VM] * (len(operands) - smem),
        out_specs=[VM] * count if count > 1 else VM,
        out_shape=out if count > 1 else out[0],
        compiler_params=params(mib),
        cost_estimate=cost(1 << 20, 1 * MIB),
    )(*operands)


def scatter_kernel(place, kept, received, own, to_one, to_two, to_three):
    size = own.shape[0]
    for away, out in enumerate((own, to_one, to_two, to_three)):
        at = pl.multiple_of(((place[1] + away) % 4) * size, size)
        out[...] = kept[pl.ds(at, size), :] + received[pl.ds(at, size), :]


def add_four_kernel(a, b, c, d, out):
    out[...] = (a[...] + b[...]) + (c[...] + d[...])


def add_two_kernel(a, b, out):
    out[...] = a[...] + b[...]


def collision_kernel(mine, theirs, high, low, out):
    size = out.shape[0]

    def times(values, which, product):
        top, rest = halves(values)
        both = product(jnp.concatenate([top, rest], axis=0), high[which])
        return both[:size] + (both[size:] + product(top, low[which]))

    moments = mine[...] + theirs[...]
    terms = times(moments, 0, dot_nt) * times(moments, 1, dot_nt)
    out[...] = times(terms, 2, dot)


def collision_part(place, kept, sent, factor_high, factor_low):
    shape = (kept.shape[0] // 4, MOMENTS)
    operands = (place, kept, exchanged(sent, 1))
    own, *others = small_call(scatter_kernel, "scatter", 4, shape, operands, 1)
    arrived = [along_y(piece, away + 1) for away, piece in enumerate(others)]
    summed = small_call(add_four_kernel, "add_four", 1, shape, (own, *arrived))
    operands = (summed, exchanged(summed, 2), factor_high, factor_low)
    share = small_call(collision_kernel, "collide", 1, shape, operands, mib=10)
    whole = small_call(add_two_kernel, "add_two", 1, shape, (share, exchanged(share, 2)))
    pieces = [whole] + [along_y(whole, away) for away in (1, 2, 3)]
    return pieces + [exchanged(piece, 1) for piece in pieces]


def relax_kernel(
    place, own, y_1, y_2, y_3, other, z_1, z_2, z_3, kind, moved, high, low,
    out, gathered, turned_high, turned_low,
):
    step = pl.program_id(0)
    size = own.shape[0]

    @pl.when(step == 0)
    def _():
        pieces = (((own, y_1, y_2, y_3), place[0]), ((other, z_1, z_2, z_3), 1 - place[0]))
        for group, core in pieces:
            for away, piece in enumerate(group):
                at = core * 4 + (place[1] + (4 - away)) % 4
                gathered[pl.ds(pl.multiple_of(at * size, size), size), :] = piece[...]
        turned_high[...], turned_low[...] = halves(gathered[...].T)

    lines = pl.ds(pl.multiple_of(step * CHUNK, CHUNK), CHUNK)
    gain = dot(high[lines, :], turned_high[...])
    gain = gain + dot(high[lines, :], turned_low[...])
    gain = gain + dot(low[lines, :], turned_high[...])
    for x in range(COLUMNS):
        fluid = HALF_STEP * (1 - kind[x : x + 1, :]).astype(F32)
        out[pl.ds(x, CHUNK, stride=COLUMNS), :] = (
            moved[x, lines, :] + fluid * gain[:, x * ROWS : (x + 1) * ROWS]
        )


def relax(place, pieces, kind, moved, high, low):
    return pl.pallas_call(
        relax_kernel,
        name="relax",
        grid=(PER_DEVICE // CHUNK,),
        in_specs=[SM] + [VM] * 12,
        out_specs=pl.BlockSpec((CHUNK * COLUMNS, ROWS), lambda i: (i, 0)),
        out_shape=jax.ShapeDtypeStruct((PER_DEVICE * COLUMNS, ROWS), F32),
        scratch_shapes=[
            pltpu.VMEM((CELLS, MOMENTS), F32),
            pltpu.VMEM((MOMENTS, CELLS), BF16),
            pltpu.VMEM((MOMENTS, CELLS), BF16),
        ],
        compiler_params=params(20),
        cost_estimate=cost(8 << 30, 16 * MIB),
    )(place, *pieces, kind, moved, high, low)


def on_device(dist, basis, left_factor, right_factor, mixing, next_cell, prev_cell, cell_kind):
    owner = lax.axis_index("vel")
    place = jnp.stack([owner % 2, owner // 4]).astype(jnp.int32)
    speed = ((MIDDLE - owner.astype(F32)) * STEP * RATIO_X).reshape(1)
    flat = dist.reshape(PER_DEVICE * COLUMNS, ROWS)
    to_right, to_left = pack(flat)
    from_left = shifted(to_right, 1)
    from_right = shifted(to_left, -1)

    given = (to_left[0, :8], left_factor, right_factor, mixing)
    factors = staged(gathered_factors, given)
    high, low, turned_high, turned_low = split_basis(basis)
    part = local_part(speed, flat, cell_kind, row_tables(next_cell, prev_cell))
    factors = split_factors(*factors)
    halo = (from_left, from_right)
    (from_left, from_right), factors = lax.optimization_barrier((halo, factors))

    moved, kept, sent = moments_part(
        speed, place, flat, part, from_left, from_right, cell_kind, high, low
    )
    pieces = collision_part(place, kept, sent, *factors)
    out = relax(place, pieces, cell_kind, moved, turned_high, turned_low)
    return out.reshape(dist.shape)


def solution(mesh):
    in_specs = (
        P("vel", "cells", None),
        P(None, "vel"),
        P("vel", None),
        P("vel", None),
        P(None, "vel"),
        P("cells", None),
        P("cells", None),
        P("cells", None),
    )
    out_specs = P("vel", "cells", None)
    return jax.shard_map(
        on_device, mesh=mesh, in_specs=in_specs, out_specs=out_specs, check_vma=False
    )
```

```python
import functools

import jax
import jax.numpy as jnp
from jax import lax
from jax.experimental import pallas as pl
from jax.experimental.pallas import tpu as pltpu
from jax.sharding import PartitionSpec as P

POINTS = 32
STEP = 6.4 / POINTS
MIDDLE = (POINTS - 1) * 0.5
RATIO_X = 0.2
RATIO_Y = 0.12
HALF_STEP = 0.5

COLUMNS = 4
ROWS = 128
PER_DEVICE = 2048
HALF = PER_DEVICE // 2
CHUNK = 256
CHUNK_M = 512
CHUNK_R = 256
MOMENTS = 512
RANKS = 1024
F32 = jnp.float32
BF16 = jnp.bfloat16
MIB = 1 << 20
UP = (0, 1, 2, 3)
DOWN = (3, 2, 1, 0)
CELLS = COLUMNS * ROWS


def shifted(x, by):
    size = lax.axis_size("cells")
    return lax.ppermute(x, "cells", [(i, (i + by) % size) for i in range(size)])


def exchanged(x, bit):
    return lax.ppermute(x, "vel", [(i, i ^ bit) for i in range(16)])


def along_y(x, by):
    return lax.ppermute(x, "vel", [(i, (i + 4 * by) % 16) for i in range(16)])


def halves(x):
    high = x.astype(BF16)
    return high, (x - high.astype(F32)).astype(BF16)


def minmod(a, b):
    return jnp.maximum(jnp.minimum(a, b), 0.0) + jnp.minimum(jnp.maximum(a, b), 0.0)


def dot(a, b):
    return jnp.dot(a, b, preferred_element_type=F32)


def dot_nt(a, b):
    return lax.dot_general(a, b, (((1,), (1,)), ((), ())), preferred_element_type=F32)


def column(ref, x, count=CHUNK):
    return ref[pl.ds(x, count, stride=COLUMNS), :]


def params(mib):
    return pltpu.CompilerParams(vmem_limit_bytes=mib * MIB)


def cost(flops, size):
    return pl.CostEstimate(flops=flops, bytes_accessed=size, transcendentals=0)


VM = pl.BlockSpec(memory_space=pltpu.VMEM)
SM = pl.BlockSpec(memory_space=pltpu.SMEM)
ANY = pl.BlockSpec(memory_space=pl.ANY)


def pack_kernel(flat, right, left, held, right_held, left_held, arrivals, leavings):
    steps = HALF // CHUNK
    rows = CHUNK * COLUMNS
    copies = []
    for i in range(steps):
        for half in range(2):
            at = pl.ds((half * steps + i) * rows, rows)
            copies.append(
                pltpu.make_async_copy(flat.at[at], held.at[at], arrivals.at[2 * i + half])
            )
    for copy in copies:
        copy.start()
    sends = []
    for i in range(steps):
        lower = held.at[pl.ds(i * rows, rows)]
        upper = held.at[pl.ds((steps + i) * rows, rows)]
        out = pl.ds(i * CHUNK, CHUNK)
        copies[2 * i].wait()
        right_held[2, out, :] = column(lower, 3)
        left_held[0, out, :] = column(lower, 0)
        left_held[1, out, :] = column(lower, 1)
        copies[2 * i + 1].wait()
        right_held[0, out, :] = column(upper, 3)
        right_held[1, out, :] = column(upper, 2)
        left_held[2, out, :] = column(upper, 0)
        for j, (source, target) in enumerate(((right_held, right), (left_held, left))):
            send = pltpu.make_async_copy(
                source.at[:, out], target.at[:, out], leavings.at[2 * i + j]
            )
            send.start()
            sends.append(send)
    for send in sends:
        send.wait()


def pack(flat):
    out = jax.ShapeDtypeStruct((3, HALF, ROWS), F32)
    return pl.pallas_call(
        pack_kernel,
        name="pack",
        in_specs=[ANY],
        out_specs=[ANY, ANY],
        out_shape=[out, out],
        scratch_shapes=[
            pltpu.VMEM((PER_DEVICE * COLUMNS, ROWS), F32),
            pltpu.VMEM((3, HALF, ROWS), F32),
            pltpu.VMEM((3, HALF, ROWS), F32),
            pltpu.SemaphoreType.DMA((2 * HALF // CHUNK,)),
            pltpu.SemaphoreType.DMA((2 * HALF // CHUNK,)),
        ],
        compiler_params=params(58),
        cost_estimate=cost(1 << 20, 8 * MIB),
    )(flat)


def staged(stage, operands):
    shapes = jax.eval_shape(stage, *operands)
    blank = lambda *_: jax.tree.map(lambda x: jnp.zeros(x.shape, x.dtype), shapes)
    taken = lax.optimization_barrier(jnp.array(True))
    return lax.cond(taken, stage, blank, *operands)


def local_kernel(speed, dist, kind, tables, out, ends):
    step = pl.program_id(0)
    in_upper = step >= HALF // CHUNK
    line = lax.broadcasted_iota(jnp.int32, (CHUNK, ROWS), 0) + step * CHUNK
    along = (line // POINTS) % POINTS
    along = jnp.where(in_upper, POINTS - 1 - along, along)
    courant_y = jnp.abs((along.astype(F32) - MIDDLE) * STEP * RATIO_Y)
    slope_y = 0.5 * (1.0 - courant_y)
    courant_x = speed[0]
    slope_x = 0.5 * (1.0 - courant_x)
    fields = []
    for x in range(COLUMNS):
        here = column(dist, x)
        both = dot(jnp.concatenate(halves(here), axis=1), tables[0, x])
        face = here + slope_y * minmod(here - both[:, :ROWS], both[:, ROWS:] - here)
        behind = dot(jnp.concatenate(halves(face), axis=1), tables[0, x, :, :ROWS])
        fields.append((here, courant_y * (face - behind)))

    def finish(order):
        here = [fields[x][0] for x in order]
        change = [fields[x][1] for x in order]
        fluid = [(1 - kind[x : x + 1, :]).astype(F32) for x in order]
        face_1 = courant_x * (here[1] + slope_x * minmod(here[1] - here[0], here[2] - here[1]))
        face_2 = courant_x * (here[2] + slope_x * minmod(here[2] - here[1], here[3] - here[2]))
        out[order[0]] = here[0] - fluid[0] * change[0]
        out[order[1]] = here[1] - fluid[1] * (change[1] + face_1)
        out[order[2]] = here[2] - fluid[2] * (change[2] + (face_2 - face_1))
        out[order[3]] = here[3] - fluid[3] * (change[3] - face_2)
        ends[0] = here[0]
        ends[1] = here[1] - here[0]
        ends[2] = here[3]
        ends[3] = here[3] - here[2]

    @pl.when(in_upper)
    def _():
        finish((0, 1, 2, 3))

    @pl.when(jnp.logical_not(in_upper))
    def _():
        finish((3, 2, 1, 0))


def local_part(speed, flat, kind, tables):
    steps = PER_DEVICE // CHUNK
    quarter = steps // 4

    def against(i):
        return jnp.where((i >= quarter) & (i < 3 * quarter), 0, 1)

    return pl.pallas_call(
        local_kernel,
        name="local_transport",
        grid=(steps,),
        in_specs=[
            SM,
            pl.BlockSpec((CHUNK * COLUMNS, ROWS), lambda i: (i, 0)),
            VM,
            pl.BlockSpec((1, COLUMNS, 2 * ROWS, 2 * ROWS), lambda i: (against(i), 0, 0, 0)),
        ],
        out_specs=[pl.BlockSpec((COLUMNS, CHUNK, ROWS), lambda i: (0, i, 0))] * 2,
        out_shape=[jax.ShapeDtypeStruct((COLUMNS, PER_DEVICE, ROWS), F32)] * 2,
        compiler_params=params(14),
        cost_estimate=cost(4 << 30, 10 * MIB),
    )(speed, flat, kind, tables)


def row_tables(following, preceding):
    rows = jnp.arange(ROWS, dtype=jnp.int32)[None, :, None]
    after = (rows == following[:, None, :]).astype(BF16)
    before = (rows == preceding[:, None, :]).astype(BF16)
    forward = jnp.concatenate([before, after], axis=2)
    backward = jnp.concatenate([after, before], axis=2)
    forward = jnp.concatenate([forward, forward], axis=1)
    backward = jnp.concatenate([backward, backward], axis=1)
    return jnp.stack([forward, backward])


def basis_kernel(basis, high, low, turned_high, turned_low):
    values = basis[...]
    high[...], low[...] = halves(values)
    turned_high[...], turned_low[...] = halves(values.T)


def split_basis(basis):
    width = 256
    half = HALF // width
    run = CHUNK_M // width

    def paired(i):
        return (i % half) // run * (2 * run) + i // half * run + i % run

    flat = pl.BlockSpec((MOMENTS, width), lambda i: (0, i))
    ordered = pl.BlockSpec((MOMENTS, width), lambda i: (0, paired(i)))
    turned = pl.BlockSpec((width, MOMENTS), lambda i: (i, 0))
    return pl.pallas_call(
        basis_kernel,
        name="split_basis",
        grid=(PER_DEVICE // width,),
        in_specs=[flat],
        out_specs=[ordered, ordered, turned, turned],
        out_shape=[jax.ShapeDtypeStruct((MOMENTS, PER_DEVICE), BF16)] * 2
        + [jax.ShapeDtypeStruct((PER_DEVICE, MOMENTS), BF16)] * 2,
        compiler_params=params(8),
        cost_estimate=cost(1 << 24, 12 * MIB),
    )(basis)


def stack_kernel(left, right, mixing, out):
    out[:128] = left[...]
    out[128:256] = right[...]
    out[256:] = mixing[...].T


def join_kernel(own, before, after, across_top, across_rest, out):
    out[0] = own[...]
    out[1] = before[...]
    out[2] = after[...]
    out[3, :192] = across_top[...]
    out[3, 192:] = across_rest[...]


def split_kernel(mine, theirs, high, low):
    for i, source in enumerate((mine, theirs)):
        for j in range(4):
            rows = pl.ds((4 * i + j) * 128, 128)
            for which in range(3):
                top, rest = halves(source[j, which * 128 : (which + 1) * 128])
                high[which, rows, :] = top
                low[which, rows, :] = rest


def gathered_factors(_, left, right, mixing):
    own = pl.pallas_call(
        stack_kernel,
        name="stack_factors",
        in_specs=[VM] * 3,
        out_specs=VM,
        out_shape=jax.ShapeDtypeStruct((384, MOMENTS), F32),
        compiler_params=params(3),
        cost_estimate=cost(1 << 20, 2 * MIB),
    )(left, right, mixing)
    before, after = along_y(own, 1), along_y(own, -1)
    across_top, across_rest = along_y(before[:192], 1), along_y(after[192:], -1)
    mine = pl.pallas_call(
        join_kernel,
        name="join_factors",
        in_specs=[VM] * 5,
        out_specs=VM,
        out_shape=jax.ShapeDtypeStruct((4, 384, MOMENTS), F32),
        compiler_params=params(8),
        cost_estimate=cost(1 << 20, 6 * MIB),
    )(own, before, after, across_top, across_rest)
    return mine, exchanged(mine, 1)


def split_factors(mine, theirs):
    out = jax.ShapeDtypeStruct((3, RANKS, MOMENTS), BF16)
    return pl.pallas_call(
        split_kernel,
        name="split_factors",
        in_specs=[VM] * 2,
        out_specs=[VM] * 2,
        out_shape=[out, out],
        compiler_params=params(16),
        cost_estimate=cost(1 << 24, 12 * MIB),
    )(mine, theirs)


def share_of_moments(high, low, values, total, out):
    step = pl.program_id(0)

    @pl.when(step == 0)
    def _():
        total[...] = jnp.zeros_like(total)

    top, rest = halves(values)
    lines = pl.ds(pl.multiple_of(step * (2 * CHUNK_M), 2 * CHUNK_M), 2 * CHUNK_M)
    added = total[...] + dot(high[:, lines], top)
    added = added + dot(high[:, lines], rest)
    added = added + dot(low[:, lines], top)
    total[...] = added

    @pl.when(step == pl.num_programs(0) - 1)
    def _():
        out[...] = total[...].T


def lines_of(which):
    step = pl.program_id(0)
    return pl.ds(pl.multiple_of(which * HALF + step * CHUNK_M, CHUNK_M), CHUNK_M)


def faces_kernel(
    speed, place, ends, part, from_left, from_right, kind, high, low, moved, sent, total
):
    courant = speed[0]
    slope = 0.5 * (1.0 - courant)
    first_core = place[0] == 0

    def half(which, order, behind, behind_two, ahead):
        lines = lines_of(which)
        fluid = [courant * (1 - kind[x : x + 1, :]).astype(F32) for x in order]
        first, forward, fourth, back = (ends[i, lines, :] for i in range(4))
        step_in = first - behind
        face_in = behind + slope * minmod(behind - behind_two, step_in)
        face_0 = first + slope * minmod(step_in, forward)
        face_3 = fourth + slope * minmod(back, ahead - fourth)
        values = {
            order[0]: part[order[0], lines, :] - fluid[0] * (face_0 - face_in),
            order[1]: part[order[1], lines, :] + fluid[1] * face_0,
            order[2]: part[order[2], lines, :],
            order[3]: part[order[3], lines, :] - fluid[3] * face_3,
        }
        for x in range(COLUMNS):
            moved[x, lines, :] = values[x]
        pair = [jnp.where(first_core, values[2 + i], values[i]) for i in range(2)]
        return jnp.concatenate(pair, axis=1)

    left, right, at = from_left, from_right, lines_of(0)
    lower = half(0, DOWN, right[0, at, :], right[1, at, :], left[2, at, :])
    upper = half(1, UP, left[0, at, :], left[1, at, :], right[2, at, :])
    share_of_moments(high, low, jnp.concatenate([lower, upper], axis=0), total, sent)


def moments_kernel(place, moved, high, low, kept, total):
    own = 2 * place[0]
    values = [
        jnp.concatenate([moved[own + i, lines_of(which), :] for i in range(2)], axis=1)
        for which in range(2)
    ]
    share_of_moments(high, low, jnp.concatenate(values, axis=0), total, kept)


def moments_part(speed, place, ends, part, from_left, from_right, kind, high, low):
    piece = jax.ShapeDtypeStruct((CELLS // 2, MOMENTS), F32)
    scratch = [pltpu.VMEM((MOMENTS, CELLS // 2), F32)]
    moved, sent = pl.pallas_call(
        faces_kernel,
        name="faces_and_moments",
        grid=(HALF // CHUNK_M,),
        in_specs=[SM, SM] + [VM] * 7,
        out_specs=[VM] * 2,
        out_shape=[jax.ShapeDtypeStruct((COLUMNS, PER_DEVICE, ROWS), F32), piece],
        scratch_shapes=scratch,
        compiler_params=params(8),
        cost_estimate=cost(4 << 30, 18 * MIB),
    )(speed, place, ends, part, from_left, from_right, kind, high, low)
    kept = pl.pallas_call(
        moments_kernel,
        name="own_moments",
        grid=(HALF // CHUNK_M,),
        in_specs=[SM] + [VM] * 3,
        out_specs=VM,
        out_shape=piece,
        scratch_shapes=scratch,
        compiler_params=params(6),
        cost_estimate=cost(4 << 30, 8 * MIB),
    )(place, moved, high, low)
    return moved, kept, sent


def small_call(kernel, name, count, shape, operands, smem=0, mib=3):
    out = [jax.ShapeDtypeStruct(shape, F32)] * count
    return pl.pallas_call(
        kernel,
        name=name,
        in_specs=[SM] * smem + [VM] * (len(operands) - smem),
        out_specs=[VM] * count if count > 1 else VM,
        out_shape=out if count > 1 else out[0],
        compiler_params=params(mib),
        cost_estimate=cost(1 << 20, 1 * MIB),
    )(*operands)


def scatter_kernel(place, kept, received, own, to_one, to_two, to_three):
    size = own.shape[0]
    for away, out in enumerate((own, to_one, to_two, to_three)):
        at = pl.multiple_of(((place[1] + away) % 4) * size, size)
        out[...] = kept[pl.ds(at, size), :] + received[pl.ds(at, size), :]


def add_four_kernel(a, b, c, d, out):
    out[...] = (a[...] + b[...]) + (c[...] + d[...])


def add_two_kernel(a, b, out):
    out[...] = a[...] + b[...]


def collision_kernel(mine, theirs, high, low, out):
    size = out.shape[0]

    def times(values, which, product):
        top, rest = halves(values)
        both = product(jnp.concatenate([top, rest], axis=0), high[which])
        return both[:size] + (both[size:] + product(top, low[which]))

    moments = mine[...] + theirs[...]
    terms = times(moments, 0, dot_nt) * times(moments, 1, dot_nt)
    out[...] = times(terms, 2, dot)


def collision_part(place, kept, sent, factor_high, factor_low):
    shape = (kept.shape[0] // 4, MOMENTS)
    operands = (place, kept, exchanged(sent, 1))
    own, *others = small_call(scatter_kernel, "scatter", 4, shape, operands, 1)
    arrived = [along_y(piece, away + 1) for away, piece in enumerate(others)]
    summed = small_call(add_four_kernel, "add_four", 1, shape, (own, *arrived))
    operands = (summed, exchanged(summed, 2), factor_high, factor_low)
    share = small_call(collision_kernel, "collide", 1, shape, operands, mib=4)
    whole = small_call(add_two_kernel, "add_two", 1, shape, (share, exchanged(share, 2)))
    pieces = [whole] + [along_y(whole, away) for away in (1, 2, 3)]
    return pieces, [exchanged(piece, 1) for piece in pieces]


def relax_kernel(
    other, place, own, y_1, y_2, y_3, kind, moved, high, low, *rest
):
    *finished, out, gathered, turned_high, turned_low = rest
    step = pl.program_id(0)
    size = own.shape[0]

    @pl.when(step == 0)
    def _():
        for away, piece in enumerate((own, y_1, y_2, y_3)):
            at = pl.multiple_of((place[1] + (4 - away)) % 4 * size, size)
            gathered[pl.ds(at, size), :] = piece[...]
        turned_high[...], turned_low[...] = halves(gathered[...].T)

    lines = pl.ds(pl.multiple_of(step * CHUNK_R, CHUNK_R), CHUNK_R)
    gain = dot(high[lines, :], turned_high[...])
    gain = gain + dot(high[lines, :], turned_low[...])
    gain = gain + dot(low[lines, :], turned_high[...])
    mine = 2 * place[0]
    here = 2 - mine if other else mine
    for i in range(2):
        fluid = HALF_STEP * (1 - kind[pl.ds(here + i, 1), :]).astype(F32)
        value = moved[here + i, lines, :] + fluid * gain[:, i * ROWS : (i + 1) * ROWS]
        if other:
            out[pl.ds(here + i, CHUNK_R, stride=COLUMNS), :] = value
            done = finished[0][i, lines, :]
            out[pl.ds(mine + i, CHUNK_R, stride=COLUMNS), :] = done
        else:
            out[i, lines, :] = value


def relax(place, pieces, kind, moved, high, low, finished=()):
    if finished:
        out_spec = pl.BlockSpec((CHUNK_R * COLUMNS, ROWS), lambda i: (i, 0))
        shape = (PER_DEVICE * COLUMNS, ROWS)
    else:
        out_spec, shape = VM, (2, PER_DEVICE, ROWS)
    return pl.pallas_call(
        functools.partial(relax_kernel, bool(finished)),
        name="relax_other" if finished else "relax_own",
        grid=(PER_DEVICE // CHUNK_R,),
        in_specs=[SM] + [VM] * (8 + len(finished)),
        out_specs=out_spec,
        out_shape=jax.ShapeDtypeStruct(shape, F32),
        scratch_shapes=[
            pltpu.VMEM((CELLS // 2, MOMENTS), F32),
            pltpu.VMEM((MOMENTS, CELLS // 2), BF16),
            pltpu.VMEM((MOMENTS, CELLS // 2), BF16),
        ],
        compiler_params=params(8),
        cost_estimate=cost(4 << 30, 12 * MIB),
    )(place, *pieces, kind, moved, high, low, *finished)


def on_device(dist, basis, left_factor, right_factor, mixing, next_cell, prev_cell, cell_kind):
    owner = lax.axis_index("vel")
    place = jnp.stack([owner % 2, owner // 4]).astype(jnp.int32)
    speed = ((MIDDLE - owner.astype(F32)) * STEP * RATIO_X).reshape(1)
    flat = dist.reshape(PER_DEVICE * COLUMNS, ROWS)
    to_right, to_left = pack(flat)
    from_left = shifted(to_right, 1)
    from_right = shifted(to_left, -1)

    given = (to_left[0, :8], left_factor, right_factor, mixing)
    factors = staged(gathered_factors, given)
    high, low, turned_high, turned_low = split_basis(basis)
    part, ends = local_part(speed, flat, cell_kind, row_tables(next_cell, prev_cell))
    factors = split_factors(*factors)
    halo = (from_left, from_right)
    (from_left, from_right), factors = lax.optimization_barrier((halo, factors))

    moved, kept, sent = moments_part(
        speed, place, ends, part, from_left, from_right, cell_kind, high, low
    )
    pieces, others = collision_part(place, kept, sent, *factors)
    finished = relax(place, pieces, cell_kind, moved, turned_high, turned_low)
    out = relax(place, others, cell_kind, moved, turned_high, turned_low, (finished,))
    return out.reshape(dist.shape)


def solution(mesh):
    in_specs = (
        P("vel", "cells", None),
        P(None, "vel"),
        P("vel", None),
        P("vel", None),
        P(None, "vel"),
        P("cells", None),
        P("cells", None),
        P("cells", None),
    )
    out_specs = P("vel", "cells", None)
    return jax.shard_map(
        on_device, mesh=mesh, in_specs=in_specs, out_specs=out_specs, check_vma=False
    )
```

```python
import functools

import jax
import jax.numpy as jnp
from jax import lax
from jax.experimental import pallas as pl
from jax.experimental.pallas import tpu as pltpu
from jax.sharding import PartitionSpec as P

POINTS = 32
STEP = 6.4 / POINTS
MIDDLE = (POINTS - 1) * 0.5
RATIO_X = 0.2
RATIO_Y = 0.12
HALF_STEP = 0.5

COLUMNS = 4
ROWS = 128
PER_DEVICE = 2048
HALF = PER_DEVICE // 2
CHUNK = 256
CHUNK_M = 1024
CHUNK_R = 1024
MOMENTS = 512
RANKS = 1024
F32 = jnp.float32
BF16 = jnp.bfloat16
MIB = 1 << 20
UP = (0, 1, 2, 3)
DOWN = (3, 2, 1, 0)
CELLS = COLUMNS * ROWS


def shifted(x, by):
    size = lax.axis_size("cells")
    return lax.ppermute(x, "cells", [(i, (i + by) % size) for i in range(size)])


def exchanged(x, bit):
    return lax.ppermute(x, "vel", [(i, i ^ bit) for i in range(16)])


def along_y(x, by):
    return lax.ppermute(x, "vel", [(i, (i + 4 * by) % 16) for i in range(16)])


def halves(x):
    high = x.astype(BF16)
    return high, (x - high.astype(F32)).astype(BF16)


def minmod(a, b):
    return jnp.maximum(jnp.minimum(a, b), 0.0) + jnp.minimum(jnp.maximum(a, b), 0.0)


def dot(a, b):
    return jnp.dot(a, b, preferred_element_type=F32)


def dot_nt(a, b):
    return lax.dot_general(a, b, (((1,), (1,)), ((), ())), preferred_element_type=F32)


def column(ref, x, count=CHUNK):
    return ref[pl.ds(x, count, stride=COLUMNS), :]


def params(mib):
    return pltpu.CompilerParams(vmem_limit_bytes=mib * MIB)


def cost(flops, size):
    return pl.CostEstimate(flops=flops, bytes_accessed=size, transcendentals=0)


VM = pl.BlockSpec(memory_space=pltpu.VMEM)
SM = pl.BlockSpec(memory_space=pltpu.SMEM)
ANY = pl.BlockSpec(memory_space=pl.ANY)


def pack_kernel(flat, right, left, held, right_held, left_held, arrivals, leavings):
    steps = HALF // CHUNK
    rows = CHUNK * COLUMNS
    copies = []
    for i in range(steps):
        for half in range(2):
            at = pl.ds((half * steps + i) * rows, rows)
            copies.append(
                pltpu.make_async_copy(flat.at[at], held.at[at], arrivals.at[2 * i + half])
            )
    for copy in copies:
        copy.start()
    sends = []
    for i in range(steps):
        lower = held.at[pl.ds(i * rows, rows)]
        upper = held.at[pl.ds((steps + i) * rows, rows)]
        out = pl.ds(i * CHUNK, CHUNK)
        copies[2 * i].wait()
        right_held[2, out, :] = column(lower, 3)
        left_held[0, out, :] = column(lower, 0)
        left_held[1, out, :] = column(lower, 1)
        copies[2 * i + 1].wait()
        right_held[0, out, :] = column(upper, 3)
        right_held[1, out, :] = column(upper, 2)
        left_held[2, out, :] = column(upper, 0)
        for j, (source, target) in enumerate(((right_held, right), (left_held, left))):
            send = pltpu.make_async_copy(
                source.at[:, out], target.at[:, out], leavings.at[2 * i + j]
            )
            send.start()
            sends.append(send)
    for send in sends:
        send.wait()


def pack(flat):
    out = jax.ShapeDtypeStruct((3, HALF, ROWS), F32)
    return pl.pallas_call(
        pack_kernel,
        name="pack",
        in_specs=[ANY],
        out_specs=[ANY, ANY],
        out_shape=[out, out],
        scratch_shapes=[
            pltpu.VMEM((PER_DEVICE * COLUMNS, ROWS), F32),
            pltpu.VMEM((3, HALF, ROWS), F32),
            pltpu.VMEM((3, HALF, ROWS), F32),
            pltpu.SemaphoreType.DMA((2 * HALF // CHUNK,)),
            pltpu.SemaphoreType.DMA((2 * HALF // CHUNK,)),
        ],
        compiler_params=params(58),
        cost_estimate=cost(1 << 20, 8 * MIB),
    )(flat)


def staged(stage, operands):
    shapes = jax.eval_shape(stage, *operands)
    blank = lambda *_: jax.tree.map(lambda x: jnp.zeros(x.shape, x.dtype), shapes)
    taken = lax.optimization_barrier(jnp.array(True))
    return lax.cond(taken, stage, blank, *operands)


def local_kernel(speed, dist, kind, tables, out, ends):
    step = pl.program_id(0)
    in_upper = step >= HALF // CHUNK
    line = lax.broadcasted_iota(jnp.int32, (CHUNK, ROWS), 0) + step * CHUNK
    along = (line // POINTS) % POINTS
    along = jnp.where(in_upper, POINTS - 1 - along, along)
    courant_y = jnp.abs((along.astype(F32) - MIDDLE) * STEP * RATIO_Y)
    slope_y = 0.5 * (1.0 - courant_y)
    courant_x = speed[0]
    slope_x = 0.5 * (1.0 - courant_x)
    fields = []
    for x in range(COLUMNS):
        here = column(dist, x)
        both = dot(jnp.concatenate(halves(here), axis=1), tables[0, x])
        face = here + slope_y * minmod(here - both[:, :ROWS], both[:, ROWS:] - here)
        behind = dot(jnp.concatenate(halves(face), axis=1), tables[0, x, :, :ROWS])
        fields.append((here, courant_y * (face - behind)))

    def finish(order):
        here = [fields[x][0] for x in order]
        change = [fields[x][1] for x in order]
        fluid = [(1 - kind[x : x + 1, :]).astype(F32) for x in order]
        face_1 = courant_x * (here[1] + slope_x * minmod(here[1] - here[0], here[2] - here[1]))
        face_2 = courant_x * (here[2] + slope_x * minmod(here[2] - here[1], here[3] - here[2]))
        out[order[0]] = here[0] - fluid[0] * change[0]
        out[order[1]] = here[1] - fluid[1] * (change[1] + face_1)
        out[order[2]] = here[2] - fluid[2] * (change[2] + (face_2 - face_1))
        out[order[3]] = here[3] - fluid[3] * (change[3] - face_2)
        ends[0] = here[0]
        ends[1] = here[1] - here[0]
        ends[2] = here[3]
        ends[3] = here[3] - here[2]

    @pl.when(in_upper)
    def _():
        finish((0, 1, 2, 3))

    @pl.when(jnp.logical_not(in_upper))
    def _():
        finish((3, 2, 1, 0))


def local_part(speed, flat, kind, tables):
    steps = PER_DEVICE // CHUNK
    quarter = steps // 4

    def against(i):
        return jnp.where((i >= quarter) & (i < 3 * quarter), 0, 1)

    return pl.pallas_call(
        local_kernel,
        name="local_transport",
        grid=(steps,),
        in_specs=[
            SM,
            pl.BlockSpec((CHUNK * COLUMNS, ROWS), lambda i: (i, 0)),
            VM,
            pl.BlockSpec((1, COLUMNS, 2 * ROWS, 2 * ROWS), lambda i: (against(i), 0, 0, 0)),
        ],
        out_specs=[pl.BlockSpec((COLUMNS, CHUNK, ROWS), lambda i: (0, i, 0))] * 2,
        out_shape=[jax.ShapeDtypeStruct((COLUMNS, PER_DEVICE, ROWS), F32)] * 2,
        compiler_params=params(14),
        cost_estimate=cost(4 << 30, 10 * MIB),
    )(speed, flat, kind, tables)


def row_tables(following, preceding):
    rows = jnp.arange(ROWS, dtype=jnp.int32)[None, :, None]
    after = (rows == following[:, None, :]).astype(BF16)
    before = (rows == preceding[:, None, :]).astype(BF16)
    forward = jnp.concatenate([before, after], axis=2)
    backward = jnp.concatenate([after, before], axis=2)
    forward = jnp.concatenate([forward, forward], axis=1)
    backward = jnp.concatenate([backward, backward], axis=1)
    return jnp.stack([forward, backward])


def basis_kernel(basis, high, low, turned_high, turned_low):
    values = basis[...]
    high[...], low[...] = halves(values)
    turned_high[...], turned_low[...] = halves(values.T)


def split_basis(basis):
    width = 256
    half = HALF // width
    run = CHUNK_M // width

    def paired(i):
        return (i % half) // run * (2 * run) + i // half * run + i % run

    flat = pl.BlockSpec((MOMENTS, width), lambda i: (0, i))
    ordered = pl.BlockSpec((MOMENTS, width), lambda i: (0, paired(i)))
    turned = pl.BlockSpec((width, MOMENTS), lambda i: (i, 0))
    return pl.pallas_call(
        basis_kernel,
        name="split_basis",
        grid=(PER_DEVICE // width,),
        in_specs=[flat],
        out_specs=[ordered, ordered, turned, turned],
        out_shape=[jax.ShapeDtypeStruct((MOMENTS, PER_DEVICE), BF16)] * 2
        + [jax.ShapeDtypeStruct((PER_DEVICE, MOMENTS), BF16)] * 2,
        compiler_params=params(8),
        cost_estimate=cost(1 << 24, 12 * MIB),
    )(basis)


def stack_kernel(left, right, mixing, out):
    out[:128] = left[...]
    out[128:256] = right[...]
    out[256:] = mixing[...].T


def join_kernel(own, before, after, across_top, across_rest, out):
    out[0] = own[...]
    out[1] = before[...]
    out[2] = after[...]
    out[3, :192] = across_top[...]
    out[3, 192:] = across_rest[...]


def split_kernel(mine, theirs, high, low):
    for i, source in enumerate((mine, theirs)):
        for j in range(4):
            rows = pl.ds((4 * i + j) * 128, 128)
            for which in range(3):
                top, rest = halves(source[j, which * 128 : (which + 1) * 128])
                high[which, rows, :] = top
                low[which, rows, :] = rest


def gathered_factors(_, left, right, mixing):
    own = pl.pallas_call(
        stack_kernel,
        name="stack_factors",
        in_specs=[VM] * 3,
        out_specs=VM,
        out_shape=jax.ShapeDtypeStruct((384, MOMENTS), F32),
        compiler_params=params(3),
        cost_estimate=cost(1 << 20, 2 * MIB),
    )(left, right, mixing)
    before, after = along_y(own, 1), along_y(own, -1)
    across_top, across_rest = along_y(before[:192], 1), along_y(after[192:], -1)
    mine = pl.pallas_call(
        join_kernel,
        name="join_factors",
        in_specs=[VM] * 5,
        out_specs=VM,
        out_shape=jax.ShapeDtypeStruct((4, 384, MOMENTS), F32),
        compiler_params=params(8),
        cost_estimate=cost(1 << 20, 6 * MIB),
    )(own, before, after, across_top, across_rest)
    return mine, exchanged(mine, 1)


def split_factors(mine, theirs):
    out = jax.ShapeDtypeStruct((3, RANKS, MOMENTS), BF16)
    return pl.pallas_call(
        split_kernel,
        name="split_factors",
        in_specs=[VM] * 2,
        out_specs=[VM] * 2,
        out_shape=[out, out],
        compiler_params=params(16),
        cost_estimate=cost(1 << 24, 12 * MIB),
    )(mine, theirs)


def share_of_moments(high, low, values, total, out):
    step = pl.program_id(0)

    @pl.when(step == 0)
    def _():
        total[...] = jnp.zeros_like(total)

    top, rest = halves(values)
    lines = pl.ds(pl.multiple_of(step * (2 * CHUNK_M), 2 * CHUNK_M), 2 * CHUNK_M)
    added = total[...] + dot(high[:, lines], top)
    added = added + dot(high[:, lines], rest)
    added = added + dot(low[:, lines], top)
    total[...] = added

    @pl.when(step == pl.num_programs(0) - 1)
    def _():
        out[...] = total[...].T


def lines_of(which):
    step = pl.program_id(0)
    return pl.ds(pl.multiple_of(which * HALF + step * CHUNK_M, CHUNK_M), CHUNK_M)


def faces_kernel(
    speed, place, ends, part, from_left, from_right, kind, high, low, moved, sent, total
):
    courant = speed[0]
    slope = 0.5 * (1.0 - courant)
    first_core = place[0] == 0

    def half(which, order, behind, behind_two, ahead):
        lines = lines_of(which)
        fluid = [courant * (1 - kind[x : x + 1, :]).astype(F32) for x in order]
        first, forward, fourth, back = (ends[i, lines, :] for i in range(4))
        step_in = first - behind
        face_in = behind + slope * minmod(behind - behind_two, step_in)
        face_0 = first + slope * minmod(step_in, forward)
        face_3 = fourth + slope * minmod(back, ahead - fourth)
        values = {
            order[0]: part[order[0], lines, :] - fluid[0] * (face_0 - face_in),
            order[1]: part[order[1], lines, :] + fluid[1] * face_0,
            order[2]: part[order[2], lines, :],
            order[3]: part[order[3], lines, :] - fluid[3] * face_3,
        }
        for x in range(COLUMNS):
            moved[x, lines, :] = values[x]
        pair = [jnp.where(first_core, values[2 + i], values[i]) for i in range(2)]
        return jnp.concatenate(pair, axis=1)

    left, right, at = from_left, from_right, lines_of(0)
    lower = half(0, DOWN, right[0, at, :], right[1, at, :], left[2, at, :])
    upper = half(1, UP, left[0, at, :], left[1, at, :], right[2, at, :])
    share_of_moments(high, low, jnp.concatenate([lower, upper], axis=0), total, sent)


def moments_kernel(place, moved, high, low, kept, total):
    own = 2 * place[0]
    values = [
        jnp.concatenate([moved[own + i, lines_of(which), :] for i in range(2)], axis=1)
        for which in range(2)
    ]
    share_of_moments(high, low, jnp.concatenate(values, axis=0), total, kept)


def moments_part(speed, place, ends, part, from_left, from_right, kind, high, low):
    piece = jax.ShapeDtypeStruct((CELLS // 2, MOMENTS), F32)
    scratch = [pltpu.VMEM((MOMENTS, CELLS // 2), F32)]
    moved, sent = pl.pallas_call(
        faces_kernel,
        name="faces_and_moments",
        grid=(HALF // CHUNK_M,),
        in_specs=[SM, SM] + [VM] * 7,
        out_specs=[VM] * 2,
        out_shape=[jax.ShapeDtypeStruct((COLUMNS, PER_DEVICE, ROWS), F32), piece],
        scratch_shapes=scratch,
        compiler_params=params(8),
        cost_estimate=cost(4 << 30, 18 * MIB),
    )(speed, place, ends, part, from_left, from_right, kind, high, low)
    kept = pl.pallas_call(
        moments_kernel,
        name="own_moments",
        grid=(HALF // CHUNK_M,),
        in_specs=[SM] + [VM] * 3,
        out_specs=VM,
        out_shape=piece,
        scratch_shapes=scratch,
        compiler_params=params(6),
        cost_estimate=cost(4 << 30, 8 * MIB),
    )(place, moved, high, low)
    return moved, kept, sent


def small_call(kernel, name, count, shape, operands, smem=0, mib=3):
    out = [jax.ShapeDtypeStruct(shape, F32)] * count
    return pl.pallas_call(
        kernel,
        name=name,
        in_specs=[SM] * smem + [VM] * (len(operands) - smem),
        out_specs=[VM] * count if count > 1 else VM,
        out_shape=out if count > 1 else out[0],
        compiler_params=params(mib),
        cost_estimate=cost(1 << 20, 1 * MIB),
    )(*operands)


def scatter_kernel(place, kept, received, own, to_one, to_two, to_three):
    size = own.shape[0]
    for away, out in enumerate((own, to_one, to_two, to_three)):
        at = pl.multiple_of(((place[1] + away) % 4) * size, size)
        out[...] = kept[pl.ds(at, size), :] + received[pl.ds(at, size), :]


def add_four_kernel(a, b, c, d, out):
    out[...] = (a[...] + b[...]) + (c[...] + d[...])


def add_two_kernel(a, b, out):
    out[...] = a[...] + b[...]


def collision_kernel(mine, theirs, high, low, out):
    size = out.shape[0]

    def times(values, which, product):
        top, rest = halves(values)
        both = product(jnp.concatenate([top, rest], axis=0), high[which])
        return both[:size] + (both[size:] + product(top, low[which]))

    moments = mine[...] + theirs[...]
    terms = times(moments, 0, dot_nt) * times(moments, 1, dot_nt)
    out[...] = times(terms, 2, dot)


def collision_part(place, kept, sent, factor_high, factor_low):
    shape = (kept.shape[0] // 4, MOMENTS)
    operands = (place, kept, exchanged(sent, 1))
    own, *others = small_call(scatter_kernel, "scatter", 4, shape, operands, 1)
    arrived = [along_y(piece, away + 1) for away, piece in enumerate(others)]
    summed = small_call(add_four_kernel, "add_four", 1, shape, (own, *arrived))
    operands = (summed, exchanged(summed, 2), factor_high, factor_low)
    share = small_call(collision_kernel, "collide", 1, shape, operands, mib=4)
    whole = small_call(add_two_kernel, "add_two", 1, shape, (share, exchanged(share, 2)))
    pieces = [whole] + [along_y(whole, away) for away in (1, 2, 3)]
    return pieces + [exchanged(piece, 1) for piece in pieces]


def relax_kernel(
    place, own, y_1, y_2, y_3, other, z_1, z_2, z_3, kind, moved, high, low,
    out, gathered, turned_high, turned_low,
):
    step = pl.program_id(0)
    size = own.shape[0]

    @pl.when(step == 0)
    def _():
        pieces = (((own, y_1, y_2, y_3), place[0]), ((other, z_1, z_2, z_3), 1 - place[0]))
        for group, core in pieces:
            for away, piece in enumerate(group):
                at = core * 4 + (place[1] + (4 - away)) % 4
                gathered[pl.ds(pl.multiple_of(at * size, size), size), :] = piece[...]
        turned_high[...], turned_low[...] = halves(gathered[...].T)

    lines = pl.ds(pl.multiple_of(step * CHUNK_R, CHUNK_R), CHUNK_R)
    gain = dot(high[lines, :], turned_high[...])
    gain = gain + dot(high[lines, :], turned_low[...])
    gain = gain + dot(low[lines, :], turned_high[...])
    for x in range(COLUMNS):
        fluid = HALF_STEP * (1 - kind[x : x + 1, :]).astype(F32)
        out[pl.ds(x, CHUNK_R, stride=COLUMNS), :] = (
            moved[x, lines, :] + fluid * gain[:, x * ROWS : (x + 1) * ROWS]
        )


def relax(place, pieces, kind, moved, high, low):
    return pl.pallas_call(
        relax_kernel,
        name="relax",
        grid=(PER_DEVICE // CHUNK_R,),
        in_specs=[SM] + [VM] * 12,
        out_specs=pl.BlockSpec((CHUNK_R * COLUMNS, ROWS), lambda i: (i, 0)),
        out_shape=jax.ShapeDtypeStruct((PER_DEVICE * COLUMNS, ROWS), F32),
        scratch_shapes=[
            pltpu.VMEM((CELLS, MOMENTS), F32),
            pltpu.VMEM((MOMENTS, CELLS), BF16),
            pltpu.VMEM((MOMENTS, CELLS), BF16),
        ],
        compiler_params=params(14),
        cost_estimate=cost(8 << 30, 16 * MIB),
    )(place, *pieces, kind, moved, high, low)


def on_device(dist, basis, left_factor, right_factor, mixing, next_cell, prev_cell, cell_kind):
    owner = lax.axis_index("vel")
    place = jnp.stack([owner % 2, owner // 4]).astype(jnp.int32)
    speed = ((MIDDLE - owner.astype(F32)) * STEP * RATIO_X).reshape(1)
    flat = dist.reshape(PER_DEVICE * COLUMNS, ROWS)
    to_right, to_left = pack(flat)
    from_left = shifted(to_right, 1)
    from_right = shifted(to_left, -1)

    given = (to_left[0, :8], left_factor, right_factor, mixing)
    factors = staged(gathered_factors, given)
    high, low, turned_high, turned_low = split_basis(basis)
    part, ends = local_part(speed, flat, cell_kind, row_tables(next_cell, prev_cell))
    factors = split_factors(*factors)
    halo = (from_left, from_right)
    (from_left, from_right), factors = lax.optimization_barrier((halo, factors))

    moved, kept, sent = moments_part(
        speed, place, ends, part, from_left, from_right, cell_kind, high, low
    )
    pieces = collision_part(place, kept, sent, *factors)
    out = relax(place, pieces, cell_kind, moved, turned_high, turned_low)
    return out.reshape(dist.shape)


def solution(mesh):
    in_specs = (
        P("vel", "cells", None),
        P(None, "vel"),
        P("vel", None),
        P("vel", None),
        P(None, "vel"),
        P("cells", None),
        P("cells", None),
        P("cells", None),
    )
    out_specs = P("vel", "cells", None)
    return jax.shard_map(
        on_device, mesh=mesh, in_specs=in_specs, out_specs=out_specs, check_vma=False
    )
```

```python
import functools

import jax
import jax.numpy as jnp
from jax import lax
from jax.experimental import pallas as pl
from jax.experimental.pallas import tpu as pltpu
from jax.sharding import PartitionSpec as P

POINTS = 32
STEP = 6.4 / POINTS
MIDDLE = (POINTS - 1) * 0.5
RATIO_X = 0.2
RATIO_Y = 0.12
HALF_STEP = 0.5

COLUMNS = 4
ROWS = 128
PER_DEVICE = 2048
HALF = PER_DEVICE // 2
CHUNK = 256
CHUNK_M = 1024
CHUNK_R = 1024
MOMENTS = 512
RANKS = 1024
F32 = jnp.float32
BF16 = jnp.bfloat16
MIB = 1 << 20
UP = (0, 1, 2, 3)
DOWN = (3, 2, 1, 0)
CELLS = COLUMNS * ROWS


def shifted(x, by):
    size = lax.axis_size("cells")
    return lax.ppermute(x, "cells", [(i, (i + by) % size) for i in range(size)])


def exchanged(x, bit):
    return lax.ppermute(x, "vel", [(i, i ^ bit) for i in range(16)])


def along_y(x, by):
    return lax.ppermute(x, "vel", [(i, (i + 4 * by) % 16) for i in range(16)])


def halves(x):
    high = x.astype(BF16)
    return high, (x - high.astype(F32)).astype(BF16)


def minmod(a, b):
    return jnp.maximum(jnp.minimum(a, b), 0.0) + jnp.minimum(jnp.maximum(a, b), 0.0)


def dot(a, b):
    return jnp.dot(a, b, preferred_element_type=F32)


def dot_nt(a, b):
    return lax.dot_general(a, b, (((1,), (1,)), ((), ())), preferred_element_type=F32)


def column(ref, x, count=CHUNK):
    return ref[pl.ds(x, count, stride=COLUMNS), :]


def params(mib):
    return pltpu.CompilerParams(vmem_limit_bytes=mib * MIB)


def cost(flops, size):
    return pl.CostEstimate(flops=flops, bytes_accessed=size, transcendentals=0)


VM = pl.BlockSpec(memory_space=pltpu.VMEM)
SM = pl.BlockSpec(memory_space=pltpu.SMEM)
ANY = pl.BlockSpec(memory_space=pl.ANY)


def pack_kernel(flat, right, left, held, right_held, left_held, arrivals, leavings):
    steps = HALF // CHUNK
    rows = CHUNK * COLUMNS
    copies = []
    for i in range(steps):
        for half in range(2):
            at = pl.ds((half * steps + i) * rows, rows)
            copies.append(
                pltpu.make_async_copy(flat.at[at], held.at[at], arrivals.at[2 * i + half])
            )
    for copy in copies:
        copy.start()
    sends = []
    for i in range(steps):
        lower = held.at[pl.ds(i * rows, rows)]
        upper = held.at[pl.ds((steps + i) * rows, rows)]
        out = pl.ds(i * CHUNK, CHUNK)
        copies[2 * i].wait()
        right_held[2, out, :] = column(lower, 3)
        left_held[0, out, :] = column(lower, 0)
        left_held[1, out, :] = column(lower, 1)
        copies[2 * i + 1].wait()
        right_held[0, out, :] = column(upper, 3)
        right_held[1, out, :] = column(upper, 2)
        left_held[2, out, :] = column(upper, 0)
        for j, (source, target) in enumerate(((right_held, right), (left_held, left))):
            send = pltpu.make_async_copy(
                source.at[:, out], target.at[:, out], leavings.at[2 * i + j]
            )
            send.start()
            sends.append(send)
    for send in sends:
        send.wait()


def pack(flat):
    out = jax.ShapeDtypeStruct((3, HALF, ROWS), F32)
    return pl.pallas_call(
        pack_kernel,
        name="pack",
        in_specs=[ANY],
        out_specs=[ANY, ANY],
        out_shape=[out, out],
        scratch_shapes=[
            pltpu.VMEM((PER_DEVICE * COLUMNS, ROWS), F32),
            pltpu.VMEM((3, HALF, ROWS), F32),
            pltpu.VMEM((3, HALF, ROWS), F32),
            pltpu.SemaphoreType.DMA((2 * HALF // CHUNK,)),
            pltpu.SemaphoreType.DMA((2 * HALF // CHUNK,)),
        ],
        compiler_params=params(58),
        cost_estimate=cost(1 << 20, 8 * MIB),
    )(flat)


def staged(stage, operands):
    shapes = jax.eval_shape(stage, *operands)
    blank = lambda *_: jax.tree.map(lambda x: jnp.zeros(x.shape, x.dtype), shapes)
    taken = lax.optimization_barrier(jnp.array(True))
    return lax.cond(taken, stage, blank, *operands)


def local_kernel(speed, dist, kind, tables, out, ends):
    step = pl.program_id(0)
    in_upper = step >= HALF // CHUNK
    line = lax.broadcasted_iota(jnp.int32, (CHUNK, ROWS), 0) + step * CHUNK
    along = (line // POINTS) % POINTS
    along = jnp.where(in_upper, POINTS - 1 - along, along)
    courant_y = jnp.abs((along.astype(F32) - MIDDLE) * STEP * RATIO_Y)
    slope_y = 0.5 * (1.0 - courant_y)
    courant_x = speed[0]
    slope_x = 0.5 * (1.0 - courant_x)
    fields = []
    for x in range(COLUMNS):
        here = column(dist, x)
        both = dot(jnp.concatenate(halves(here), axis=1), tables[0, x])
        face = here + slope_y * minmod(here - both[:, :ROWS], both[:, ROWS:] - here)
        behind = dot(jnp.concatenate(halves(face), axis=1), tables[0, x, :, :ROWS])
        fields.append((here, courant_y * (face - behind)))

    def finish(order):
        here = [fields[x][0] for x in order]
        change = [fields[x][1] for x in order]
        fluid = [(1 - kind[x : x + 1, :]).astype(F32) for x in order]
        face_1 = courant_x * (here[1] + slope_x * minmod(here[1] - here[0], here[2] - here[1]))
        face_2 = courant_x * (here[2] + slope_x * minmod(here[2] - here[1], here[3] - here[2]))
        out[order[0]] = here[0] - fluid[0] * change[0]
        out[order[1]] = here[1] - fluid[1] * (change[1] + face_1)
        out[order[2]] = here[2] - fluid[2] * (change[2] + (face_2 - face_1))
        out[order[3]] = here[3] - fluid[3] * (change[3] - face_2)
        ends[0] = here[0]
        ends[1] = here[1] - here[0]
        ends[2] = here[3]
        ends[3] = here[3] - here[2]

    @pl.when(in_upper)
    def _():
        finish((0, 1, 2, 3))

    @pl.when(jnp.logical_not(in_upper))
    def _():
        finish((3, 2, 1, 0))


def local_part(speed, flat, kind, tables):
    steps = PER_DEVICE // CHUNK
    quarter = steps // 4

    def against(i):
        return jnp.where((i >= quarter) & (i < 3 * quarter), 0, 1)

    return pl.pallas_call(
        local_kernel,
        name="local_transport",
        grid=(steps,),
        in_specs=[
            SM,
            pl.BlockSpec((CHUNK * COLUMNS, ROWS), lambda i: (i, 0)),
            VM,
            pl.BlockSpec((1, COLUMNS, 2 * ROWS, 2 * ROWS), lambda i: (against(i), 0, 0, 0)),
        ],
        out_specs=[pl.BlockSpec((COLUMNS, CHUNK, ROWS), lambda i: (0, i, 0))] * 2,
        out_shape=[jax.ShapeDtypeStruct((COLUMNS, PER_DEVICE, ROWS), F32)] * 2,
        compiler_params=params(14),
        cost_estimate=cost(4 << 30, 10 * MIB),
    )(speed, flat, kind, tables)


def row_tables(following, preceding):
    rows = jnp.arange(ROWS, dtype=jnp.int32)[None, :, None]
    after = (rows == following[:, None, :]).astype(BF16)
    before = (rows == preceding[:, None, :]).astype(BF16)
    forward = jnp.concatenate([before, after], axis=2)
    backward = jnp.concatenate([after, before], axis=2)
    forward = jnp.concatenate([forward, forward], axis=1)
    backward = jnp.concatenate([backward, backward], axis=1)
    return jnp.stack([forward, backward])


def basis_kernel(basis, high, low, turned_high, turned_low):
    values = basis[...]
    high[...], low[...] = halves(values)
    turned_high[...], turned_low[...] = halves(values.T)


def split_basis(basis):
    width = 256
    half = HALF // width
    run = CHUNK_M // width

    def paired(i):
        return (i % half) // run * (2 * run) + i // half * run + i % run

    flat = pl.BlockSpec((MOMENTS, width), lambda i: (0, i))
    ordered = pl.BlockSpec((MOMENTS, width), lambda i: (0, paired(i)))
    turned = pl.BlockSpec((width, MOMENTS), lambda i: (i, 0))
    return pl.pallas_call(
        basis_kernel,
        name="split_basis",
        grid=(PER_DEVICE // width,),
        in_specs=[flat],
        out_specs=[ordered, ordered, turned, turned],
        out_shape=[jax.ShapeDtypeStruct((MOMENTS, PER_DEVICE), BF16)] * 2
        + [jax.ShapeDtypeStruct((PER_DEVICE, MOMENTS), BF16)] * 2,
        compiler_params=params(8),
        cost_estimate=cost(1 << 24, 12 * MIB),
    )(basis)


def stack_kernel(left, right, mixing, out):
    out[:128] = left[...]
    out[128:256] = right[...]
    out[256:] = mixing[...].T


def join_kernel(own, before, after, across_top, across_rest, out):
    out[0] = own[...]
    out[1] = before[...]
    out[2] = after[...]
    out[3, :192] = across_top[...]
    out[3, 192:] = across_rest[...]


def split_kernel(mine, theirs, high, low):
    for i, source in enumerate((mine, theirs)):
        for j in range(4):
            rows = pl.ds((4 * i + j) * 128, 128)
            for which in range(3):
                top, rest = halves(source[j, which * 128 : (which + 1) * 128])
                high[which, rows, :] = top
                low[which, rows, :] = rest


def gathered_factors(_, left, right, mixing):
    own = pl.pallas_call(
        stack_kernel,
        name="stack_factors",
        in_specs=[VM] * 3,
        out_specs=VM,
        out_shape=jax.ShapeDtypeStruct((384, MOMENTS), F32),
        compiler_params=params(3),
        cost_estimate=cost(1 << 20, 2 * MIB),
    )(left, right, mixing)
    before, after = along_y(own, 1), along_y(own, -1)
    across_top, across_rest = along_y(before[:192], 1), along_y(after[192:], -1)
    mine = pl.pallas_call(
        join_kernel,
        name="join_factors",
        in_specs=[VM] * 5,
        out_specs=VM,
        out_shape=jax.ShapeDtypeStruct((4, 384, MOMENTS), F32),
        compiler_params=params(8),
        cost_estimate=cost(1 << 20, 6 * MIB),
    )(own, before, after, across_top, across_rest)
    return mine, exchanged(mine, 1)


def split_factors(mine, theirs):
    out = jax.ShapeDtypeStruct((3, RANKS, MOMENTS), BF16)
    return pl.pallas_call(
        split_kernel,
        name="split_factors",
        in_specs=[VM] * 2,
        out_specs=[VM] * 2,
        out_shape=[out, out],
        compiler_params=params(16),
        cost_estimate=cost(1 << 24, 12 * MIB),
    )(mine, theirs)


def share_of_moments(high, low, values, total, out):
    step = pl.program_id(0)

    @pl.when(step == 0)
    def _():
        total[...] = jnp.zeros_like(total)

    top, rest = halves(values)
    lines = pl.ds(pl.multiple_of(step * (2 * CHUNK_M), 2 * CHUNK_M), 2 * CHUNK_M)
    added = total[...] + dot(high[:, lines], top)
    added = added + dot(high[:, lines], rest)
    added = added + dot(low[:, lines], top)
    total[...] = added

    @pl.when(step == pl.num_programs(0) - 1)
    def _():
        out[...] = total[...].T


def lines_of(which):
    step = pl.program_id(0)
    return pl.ds(pl.multiple_of(which * HALF + step * CHUNK_M, CHUNK_M), CHUNK_M)


def faces_kernel(
    speed, place, ends, part, from_left, from_right, kind, high, low, moved, sent, total
):
    courant = speed[0]
    slope = 0.5 * (1.0 - courant)
    first_core = place[0] == 0

    def half(which, order, behind, behind_two, ahead):
        lines = lines_of(which)
        fluid = [courant * (1 - kind[x : x + 1, :]).astype(F32) for x in order]
        first, forward, fourth, back = (ends[i, lines, :] for i in range(4))
        step_in = first - behind
        face_in = behind + slope * minmod(behind - behind_two, step_in)
        face_0 = first + slope * minmod(step_in, forward)
        face_3 = fourth + slope * minmod(back, ahead - fourth)
        values = {
            order[0]: part[order[0], lines, :] - fluid[0] * (face_0 - face_in),
            order[1]: part[order[1], lines, :] + fluid[1] * face_0,
            order[2]: part[order[2], lines, :],
            order[3]: part[order[3], lines, :] - fluid[3] * face_3,
        }
        for x in range(COLUMNS):
            moved[x, lines, :] = values[x]
        pair = [jnp.where(first_core, values[2 + i], values[i]) for i in range(2)]
        return jnp.concatenate(pair, axis=1)

    left, right, at = from_left, from_right, lines_of(0)
    lower = half(0, DOWN, right[0, at, :], right[1, at, :], left[2, at, :])
    upper = half(1, UP, left[0, at, :], left[1, at, :], right[2, at, :])
    share_of_moments(high, low, jnp.concatenate([lower, upper], axis=0), total, sent)


def moments_kernel(place, moved, high, low, kept, total):
    own = 2 * place[0]
    values = [
        jnp.concatenate([moved[own + i, lines_of(which), :] for i in range(2)], axis=1)
        for which in range(2)
    ]
    share_of_moments(high, low, jnp.concatenate(values, axis=0), total, kept)


def moments_part(speed, place, ends, part, from_left, from_right, kind, high, low):
    piece = jax.ShapeDtypeStruct((CELLS // 2, MOMENTS), F32)
    scratch = [pltpu.VMEM((MOMENTS, CELLS // 2), F32)]
    moved, sent = pl.pallas_call(
        faces_kernel,
        name="faces_and_moments",
        grid=(HALF // CHUNK_M,),
        in_specs=[SM, SM] + [VM] * 7,
        out_specs=[VM] * 2,
        out_shape=[jax.ShapeDtypeStruct((COLUMNS, PER_DEVICE, ROWS), F32), piece],
        scratch_shapes=scratch,
        compiler_params=params(8),
        cost_estimate=cost(4 << 30, 18 * MIB),
    )(speed, place, ends, part, from_left, from_right, kind, high, low)
    kept = pl.pallas_call(
        moments_kernel,
        name="own_moments",
        grid=(HALF // CHUNK_M,),
        in_specs=[SM] + [VM] * 3,
        out_specs=VM,
        out_shape=piece,
        scratch_shapes=scratch,
        compiler_params=params(6),
        cost_estimate=cost(4 << 30, 8 * MIB),
    )(place, moved, high, low)
    return moved, kept, sent


def small_call(kernel, name, count, shape, operands, smem=0, mib=3):
    out = [jax.ShapeDtypeStruct(shape, F32)] * count
    return pl.pallas_call(
        kernel,
        name=name,
        in_specs=[SM] * smem + [VM] * (len(operands) - smem),
        out_specs=[VM] * count if count > 1 else VM,
        out_shape=out if count > 1 else out[0],
        compiler_params=params(mib),
        cost_estimate=cost(1 << 20, 1 * MIB),
    )(*operands)


def scatter_kernel(place, kept, received, own, to_one, to_two, to_three):
    size = own.shape[0]
    for away, out in enumerate((own, to_one, to_two, to_three)):
        at = pl.multiple_of(((place[1] + away) % 4) * size, size)
        out[...] = kept[pl.ds(at, size), :] + received[pl.ds(at, size), :]


def add_four_kernel(a, b, c, d, upper, lower):
    total = (a[...] + b[...]) + (c[...] + d[...])
    upper[...], lower[...] = total[:32], total[32:]


def add_two_kernel(a, b, c, d, out):
    out[:32] = a[...] + c[...]
    out[32:] = b[...] + d[...]


def collision_kernel(mine_a, mine_b, theirs_a, theirs_b, high, low, upper, lower):
    def times(values, which, product):
        top, rest = halves(values)
        both = product(jnp.concatenate([top, rest], axis=0), high[which])
        return both[:64] + (both[64:] + product(top, low[which]))

    parts = [mine_a[...] + theirs_a[...], mine_b[...] + theirs_b[...]]
    moments = jnp.concatenate(parts, axis=0)
    terms = times(moments, 0, dot_nt) * times(moments, 1, dot_nt)
    result = times(terms, 2, dot)
    upper[...], lower[...] = result[:32], result[32:]


def collision_part(place, kept, sent, factor_high, factor_low):
    shape, half = (64, MOMENTS), (32, MOMENTS)
    operands = (place, kept, exchanged(sent, 1))
    own, to_one, to_two, to_three = small_call(scatter_kernel, "scatter", 4, shape, operands, 1)
    arrived = (along_y(to_two, 2), along_y(to_three, 3), along_y(to_one, 1))
    mine = small_call(add_four_kernel, "add_four", 2, half, (own, *arrived))
    theirs = [exchanged(piece, 2) for piece in mine]
    operands = (*mine, *theirs, factor_high, factor_low)
    mine = small_call(collision_kernel, "collide", 2, half, operands, mib=4)
    theirs = [exchanged(piece, 2) for piece in mine]
    whole = small_call(add_two_kernel, "add_two", 1, shape, (*mine, *theirs))
    y_2, y_1, y_3 = (along_y(whole, away) for away in (2, 1, 3))
    pieces = [whole, y_1, y_3, y_2]
    return pieces + [exchanged(piece, 1) for piece in pieces]


def relax_kernel(
    place, own, y_1, y_3, y_2, other, z_1, z_3, z_2, kind, moved, high, low,
    out, gathered, turned_high, turned_low,
):
    step = pl.program_id(0)
    size = own.shape[0]

    @pl.when(step == 0)
    def _():
        pieces = (((own, y_1, y_2, y_3), place[0]), ((other, z_1, z_2, z_3), 1 - place[0]))
        for group, core in pieces:
            for away, piece in enumerate(group):
                at = core * 4 + (place[1] + (4 - away)) % 4
                gathered[pl.ds(pl.multiple_of(at * size, size), size), :] = piece[...]
        turned_high[...], turned_low[...] = halves(gathered[...].T)

    lines = pl.ds(pl.multiple_of(step * CHUNK_R, CHUNK_R), CHUNK_R)
    gain = dot(high[lines, :], turned_high[...])
    gain = gain + dot(high[lines, :], turned_low[...])
    gain = gain + dot(low[lines, :], turned_high[...])
    for x in range(COLUMNS):
        fluid = HALF_STEP * (1 - kind[x : x + 1, :]).astype(F32)
        out[pl.ds(x, CHUNK_R, stride=COLUMNS), :] = (
            moved[x, lines, :] + fluid * gain[:, x * ROWS : (x + 1) * ROWS]
        )


def relax(place, pieces, kind, moved, high, low):
    return pl.pallas_call(
        relax_kernel,
        name="relax",
        grid=(PER_DEVICE // CHUNK_R,),
        in_specs=[SM] + [VM] * 12,
        out_specs=pl.BlockSpec((CHUNK_R * COLUMNS, ROWS), lambda i: (i, 0)),
        out_shape=jax.ShapeDtypeStruct((PER_DEVICE * COLUMNS, ROWS), F32),
        scratch_shapes=[
            pltpu.VMEM((CELLS, MOMENTS), F32),
            pltpu.VMEM((MOMENTS, CELLS), BF16),
            pltpu.VMEM((MOMENTS, CELLS), BF16),
        ],
        compiler_params=params(14),
        cost_estimate=cost(8 << 30, 16 * MIB),
    )(place, *pieces, kind, moved, high, low)


def on_device(dist, basis, left_factor, right_factor, mixing, next_cell, prev_cell, cell_kind):
    owner = lax.axis_index("vel")
    place = jnp.stack([owner % 2, owner // 4]).astype(jnp.int32)
    speed = ((MIDDLE - owner.astype(F32)) * STEP * RATIO_X).reshape(1)
    flat = dist.reshape(PER_DEVICE * COLUMNS, ROWS)
    to_right, to_left = pack(flat)
    from_left = shifted(to_right, 1)
    from_right = shifted(to_left, -1)

    given = (to_left[0, :8], left_factor, right_factor, mixing)
    factors = staged(gathered_factors, given)
    high, low, turned_high, turned_low = split_basis(basis)
    part, ends = local_part(speed, flat, cell_kind, row_tables(next_cell, prev_cell))
    factors = split_factors(*factors)
    halo = (from_left, from_right)
    (from_left, from_right), factors = lax.optimization_barrier((halo, factors))

    moved, kept, sent = moments_part(
        speed, place, ends, part, from_left, from_right, cell_kind, high, low
    )
    pieces = collision_part(place, kept, sent, *factors)
    out = relax(place, pieces, cell_kind, moved, turned_high, turned_low)
    return out.reshape(dist.shape)


def solution(mesh):
    in_specs = (
        P("vel", "cells", None),
        P(None, "vel"),
        P("vel", None),
        P("vel", None),
        P(None, "vel"),
        P("cells", None),
        P("cells", None),
        P("cells", None),
    )
    out_specs = P("vel", "cells", None)
    return jax.shard_map(
        on_device, mesh=mesh, in_specs=in_specs, out_specs=out_specs, check_vma=False
    )
```

```python
import functools

import jax
import jax.numpy as jnp
from jax import lax
from jax.experimental import pallas as pl
from jax.experimental.pallas import tpu as pltpu
from jax.sharding import PartitionSpec as P

POINTS = 32
STEP = 6.4 / POINTS
MIDDLE = (POINTS - 1) * 0.5
RATIO_X = 0.2
RATIO_Y = 0.12
HALF_STEP = 0.5

COLUMNS = 4
ROWS = 128
PER_DEVICE = 2048
HALF = PER_DEVICE // 2
CHUNK = 256
CHUNK_M = 1024
MOMENTS = 512
RANKS = 1024
F32 = jnp.float32
BF16 = jnp.bfloat16
MIB = 1 << 20
UP = (0, 1, 2, 3)
DOWN = (3, 2, 1, 0)
CELLS = COLUMNS * ROWS


def shifted(x, by):
    size = lax.axis_size("cells")
    return lax.ppermute(x, "cells", [(i, (i + by) % size) for i in range(size)])


def exchanged(x, bit):
    return lax.ppermute(x, "vel", [(i, i ^ bit) for i in range(16)])


def along_y(x, by):
    return lax.ppermute(x, "vel", [(i, (i + 4 * by) % 16) for i in range(16)])


def halves(x):
    high = x.astype(BF16)
    return high, (x - high.astype(F32)).astype(BF16)


def minmod(a, b):
    return jnp.maximum(jnp.minimum(a, b), 0.0) + jnp.minimum(jnp.maximum(a, b), 0.0)


def dot(a, b):
    return jnp.dot(a, b, preferred_element_type=F32)


def dot_nt(a, b):
    return lax.dot_general(a, b, (((1,), (1,)), ((), ())), preferred_element_type=F32)


def column(ref, x, count=CHUNK):
    return ref[pl.ds(x, count, stride=COLUMNS), :]


def params(mib):
    return pltpu.CompilerParams(vmem_limit_bytes=mib * MIB)


def cost(flops, size):
    return pl.CostEstimate(flops=flops, bytes_accessed=size, transcendentals=0)


VM = pl.BlockSpec(memory_space=pltpu.VMEM)
SM = pl.BlockSpec(memory_space=pltpu.SMEM)
ANY = pl.BlockSpec(memory_space=pl.ANY)


def pack_kernel(flat, right, left, held, right_held, left_held, arrivals, leavings):
    steps = HALF // CHUNK
    rows = CHUNK * COLUMNS
    copies = []
    for i in range(steps):
        for half in range(2):
            at = pl.ds((half * steps + i) * rows, rows)
            copies.append(
                pltpu.make_async_copy(flat.at[at], held.at[at], arrivals.at[2 * i + half])
            )
    for copy in copies:
        copy.start()
    sends = []
    for i in range(steps):
        lower = held.at[pl.ds(i * rows, rows)]
        upper = held.at[pl.ds((steps + i) * rows, rows)]
        out = pl.ds(i * CHUNK, CHUNK)
        copies[2 * i].wait()
        right_held[2, out, :] = column(lower, 3)
        left_held[0, out, :] = column(lower, 0)
        left_held[1, out, :] = column(lower, 1)
        copies[2 * i + 1].wait()
        right_held[0, out, :] = column(upper, 3)
        right_held[1, out, :] = column(upper, 2)
        left_held[2, out, :] = column(upper, 0)
        for j, (source, target) in enumerate(((right_held, right), (left_held, left))):
            send = pltpu.make_async_copy(
                source.at[:, out], target.at[:, out], leavings.at[2 * i + j]
            )
            send.start()
            sends.append(send)
    for send in sends:
        send.wait()


def pack(flat):
    out = jax.ShapeDtypeStruct((3, HALF, ROWS), F32)
    return pl.pallas_call(
        pack_kernel,
        name="pack",
        in_specs=[ANY],
        out_specs=[ANY, ANY],
        out_shape=[out, out],
        scratch_shapes=[
            pltpu.VMEM((PER_DEVICE * COLUMNS, ROWS), F32),
            pltpu.VMEM((3, HALF, ROWS), F32),
            pltpu.VMEM((3, HALF, ROWS), F32),
            pltpu.SemaphoreType.DMA((2 * HALF // CHUNK,)),
            pltpu.SemaphoreType.DMA((2 * HALF // CHUNK,)),
        ],
        compiler_params=params(58),
        cost_estimate=cost(1 << 20, 8 * MIB),
    )(flat)


def staged(stage, operands):
    shapes = jax.eval_shape(stage, *operands)
    blank = lambda *_: jax.tree.map(lambda x: jnp.zeros(x.shape, x.dtype), shapes)
    taken = lax.optimization_barrier(jnp.array(True))
    return lax.cond(taken, stage, blank, *operands)


def local_kernel(speed, dist, kind, tables, out, ends):
    step = pl.program_id(0)
    in_upper = step >= HALF // CHUNK
    line = lax.broadcasted_iota(jnp.int32, (CHUNK, ROWS), 0) + step * CHUNK
    along = (line // POINTS) % POINTS
    along = jnp.where(in_upper, POINTS - 1 - along, along)
    courant_y = jnp.abs((along.astype(F32) - MIDDLE) * STEP * RATIO_Y)
    slope_y = 0.5 * (1.0 - courant_y)
    courant_x = speed[0]
    slope_x = 0.5 * (1.0 - courant_x)
    fields = []
    for x in range(COLUMNS):
        here = column(dist, x)
        both = dot(jnp.concatenate(halves(here), axis=1), tables[0, x])
        face = here + slope_y * minmod(here - both[:, :ROWS], both[:, ROWS:] - here)
        behind = dot(jnp.concatenate(halves(face), axis=1), tables[0, x, :, :ROWS])
        fields.append((here, courant_y * (face - behind)))

    def finish(order):
        here = [fields[x][0] for x in order]
        change = [fields[x][1] for x in order]
        fluid = [(1 - kind[x : x + 1, :]).astype(F32) for x in order]
        face_1 = courant_x * (here[1] + slope_x * minmod(here[1] - here[0], here[2] - here[1]))
        face_2 = courant_x * (here[2] + slope_x * minmod(here[2] - here[1], here[3] - here[2]))
        out[order[0]] = here[0] - fluid[0] * change[0]
        out[order[1]] = here[1] - fluid[1] * (change[1] + face_1)
        out[order[2]] = here[2] - fluid[2] * (change[2] + (face_2 - face_1))
        out[order[3]] = here[3] - fluid[3] * (change[3] - face_2)
        ends[0] = here[0]
        ends[1] = here[1] - here[0]
        ends[2] = here[3]
        ends[3] = here[3] - here[2]

    @pl.when(in_upper)
    def _():
        finish((0, 1, 2, 3))

    @pl.when(jnp.logical_not(in_upper))
    def _():
        finish((3, 2, 1, 0))


def local_part(speed, flat, kind, tables):
    steps = PER_DEVICE // CHUNK
    quarter = steps // 4

    def against(i):
        return jnp.where((i >= quarter) & (i < 3 * quarter), 0, 1)

    return pl.pallas_call(
        local_kernel,
        name="local_transport",
        grid=(steps,),
        in_specs=[
            SM,
            pl.BlockSpec((CHUNK * COLUMNS, ROWS), lambda i: (i, 0)),
            VM,
            pl.BlockSpec((1, COLUMNS, 2 * ROWS, 2 * ROWS), lambda i: (against(i), 0, 0, 0)),
        ],
        out_specs=[pl.BlockSpec((COLUMNS, CHUNK, ROWS), lambda i: (0, i, 0))] * 2,
        out_shape=[jax.ShapeDtypeStruct((COLUMNS, PER_DEVICE, ROWS), F32)] * 2,
        compiler_params=params(14),
        cost_estimate=cost(4 << 30, 10 * MIB),
    )(speed, flat, kind, tables)


def row_tables(following, preceding):
    rows = jnp.arange(ROWS, dtype=jnp.int32)[None, :, None]
    after = (rows == following[:, None, :]).astype(BF16)
    before = (rows == preceding[:, None, :]).astype(BF16)
    forward = jnp.concatenate([before, after], axis=2)
    backward = jnp.concatenate([after, before], axis=2)
    forward = jnp.concatenate([forward, forward], axis=1)
    backward = jnp.concatenate([backward, backward], axis=1)
    return jnp.stack([forward, backward])


def basis_kernel(basis, high, low, turned_high, turned_low):
    values = basis[...]
    high[...], low[...] = halves(values)
    turned_high[...], turned_low[...] = halves(values.T)


def split_basis(basis):
    width = 256
    half = HALF // width
    run = CHUNK_M // width

    def paired(i):
        return (i % half) // run * (2 * run) + i // half * run + i % run

    flat = pl.BlockSpec((MOMENTS, width), lambda i: (0, i))
    ordered = pl.BlockSpec((MOMENTS, width), lambda i: (0, paired(i)))
    turned = pl.BlockSpec((width, MOMENTS), lambda i: (i, 0))
    return pl.pallas_call(
        basis_kernel,
        name="split_basis",
        grid=(PER_DEVICE // width,),
        in_specs=[flat],
        out_specs=[ordered, ordered, turned, turned],
        out_shape=[jax.ShapeDtypeStruct((MOMENTS, PER_DEVICE), BF16)] * 2
        + [jax.ShapeDtypeStruct((PER_DEVICE, MOMENTS), BF16)] * 2,
        compiler_params=params(8),
        cost_estimate=cost(1 << 24, 12 * MIB),
    )(basis)


def stack_kernel(left, right, mixing, out):
    out[:128] = left[...]
    out[128:256] = right[...]
    out[256:] = mixing[...].T


def join_kernel(own, before, after, across_top, across_rest, out):
    out[0] = own[...]
    out[1] = before[...]
    out[2] = after[...]
    out[3, :192] = across_top[...]
    out[3, 192:] = across_rest[...]


def split_kernel(mine, theirs, high, low):
    for i, source in enumerate((mine, theirs)):
        for j in range(4):
            rows = pl.ds((4 * i + j) * 128, 128)
            for which in range(3):
                top, rest = halves(source[j, which * 128 : (which + 1) * 128])
                high[which, rows, :] = top
                low[which, rows, :] = rest


def gathered_factors(_, left, right, mixing):
    own = pl.pallas_call(
        stack_kernel,
        name="stack_factors",
        in_specs=[VM] * 3,
        out_specs=VM,
        out_shape=jax.ShapeDtypeStruct((384, MOMENTS), F32),
        compiler_params=params(3),
        cost_estimate=cost(1 << 20, 2 * MIB),
    )(left, right, mixing)
    before, after = along_y(own, 1), along_y(own, -1)
    across_top, across_rest = along_y(before[:192], 1), along_y(after[192:], -1)
    mine = pl.pallas_call(
        join_kernel,
        name="join_factors",
        in_specs=[VM] * 5,
        out_specs=VM,
        out_shape=jax.ShapeDtypeStruct((4, 384, MOMENTS), F32),
        compiler_params=params(8),
        cost_estimate=cost(1 << 20, 6 * MIB),
    )(own, before, after, across_top, across_rest)
    return mine, exchanged(mine, 1)


def split_factors(mine, theirs):
    out = jax.ShapeDtypeStruct((3, RANKS, MOMENTS), BF16)
    return pl.pallas_call(
        split_kernel,
        name="split_factors",
        in_specs=[VM] * 2,
        out_specs=[VM] * 2,
        out_shape=[out, out],
        compiler_params=params(16),
        cost_estimate=cost(1 << 24, 12 * MIB),
    )(mine, theirs)


def share_of_moments(high, low, values, total, out):
    step = pl.program_id(0)

    @pl.when(step == 0)
    def _():
        total[...] = jnp.zeros_like(total)

    top, rest = halves(values)
    lines = pl.ds(pl.multiple_of(step * (2 * CHUNK_M), 2 * CHUNK_M), 2 * CHUNK_M)
    added = total[...] + dot(high[:, lines], top)
    added = added + dot(high[:, lines], rest)
    added = added + dot(low[:, lines], top)
    total[...] = added

    @pl.when(step == pl.num_programs(0) - 1)
    def _():
        out[...] = total[...].T


def lines_of(which):
    step = pl.program_id(0)
    return pl.ds(pl.multiple_of(which * HALF + step * CHUNK_M, CHUNK_M), CHUNK_M)


def faces_kernel(
    speed, place, ends, part, from_left, from_right, kind, high, low, moved, sent, total
):
    courant = speed[0]
    slope = 0.5 * (1.0 - courant)
    first_core = place[0] == 0

    def half(which, order, behind, behind_two, ahead):
        lines = lines_of(which)
        fluid = [courant * (1 - kind[x : x + 1, :]).astype(F32) for x in order]
        first, forward, fourth, back = (ends[i, lines, :] for i in range(4))
        step_in = first - behind
        face_in = behind + slope * minmod(behind - behind_two, step_in)
        face_0 = first + slope * minmod(step_in, forward)
        face_3 = fourth + slope * minmod(back, ahead - fourth)
        values = {
            order[0]: part[order[0], lines, :] - fluid[0] * (face_0 - face_in),
            order[1]: part[order[1], lines, :] + fluid[1] * face_0,
            order[2]: part[order[2], lines, :],
            order[3]: part[order[3], lines, :] - fluid[3] * face_3,
        }
        for x in range(COLUMNS):
            moved[x, lines, :] = values[x]
        pair = [jnp.where(first_core, values[2 + i], values[i]) for i in range(2)]
        return jnp.concatenate(pair, axis=1)

    left, right, at = from_left, from_right, lines_of(0)
    lower = half(0, DOWN, right[0, at, :], right[1, at, :], left[2, at, :])
    upper = half(1, UP, left[0, at, :], left[1, at, :], right[2, at, :])
    share_of_moments(high, low, jnp.concatenate([lower, upper], axis=0), total, sent)


def moments_kernel(place, moved, high, low, kept, total):
    own = 2 * place[0]
    values = [
        jnp.concatenate([moved[own + i, lines_of(which), :] for i in range(2)], axis=1)
        for which in range(2)
    ]
    share_of_moments(high, low, jnp.concatenate(values, axis=0), total, kept)


def moments_part(speed, place, ends, part, from_left, from_right, kind, high, low):
    piece = jax.ShapeDtypeStruct((CELLS // 2, MOMENTS), F32)
    scratch = [pltpu.VMEM((MOMENTS, CELLS // 2), F32)]
    moved, sent = pl.pallas_call(
        faces_kernel,
        name="faces_and_moments",
        grid=(HALF // CHUNK_M,),
        in_specs=[SM, SM] + [VM] * 7,
        out_specs=[VM] * 2,
        out_shape=[jax.ShapeDtypeStruct((COLUMNS, PER_DEVICE, ROWS), F32), piece],
        scratch_shapes=scratch,
        compiler_params=params(8),
        cost_estimate=cost(4 << 30, 18 * MIB),
    )(speed, place, ends, part, from_left, from_right, kind, high, low)
    kept = pl.pallas_call(
        moments_kernel,
        name="own_moments",
        grid=(HALF // CHUNK_M,),
        in_specs=[SM] + [VM] * 3,
        out_specs=VM,
        out_shape=piece,
        scratch_shapes=scratch,
        compiler_params=params(6),
        cost_estimate=cost(4 << 30, 8 * MIB),
    )(place, moved, high, low)
    return moved, kept, sent


def small_call(kernel, name, count, shape, operands, smem=0, mib=3):
    out = [jax.ShapeDtypeStruct(shape, F32)] * count
    return pl.pallas_call(
        kernel,
        name=name,
        in_specs=[SM] * smem + [VM] * (len(operands) - smem),
        out_specs=[VM] * count if count > 1 else VM,
        out_shape=out if count > 1 else out[0],
        compiler_params=params(mib),
        cost_estimate=cost(1 << 20, 1 * MIB),
    )(*operands)


def scatter_kernel(place, kept, received, own, to_one, to_two, to_three):
    size = own.shape[0]
    for away, out in enumerate((own, to_one, to_two, to_three)):
        at = pl.multiple_of(((place[1] + away) % 4) * size, size)
        out[...] = kept[pl.ds(at, size), :] + received[pl.ds(at, size), :]


def add_four_kernel(a, b, c, d, out):
    out[...] = (a[...] + b[...]) + (c[...] + d[...])


def add_two_kernel(a, b, out):
    out[...] = a[...] + b[...]


def collision_kernel(mine, theirs, high, low, out):
    size = out.shape[0]

    def times(values, which, product):
        top, rest = halves(values)
        both = product(jnp.concatenate([top, rest], axis=0), high[which])
        return both[:size] + (both[size:] + product(top, low[which]))

    moments = mine[...] + theirs[...]
    terms = times(moments, 0, dot_nt) * times(moments, 1, dot_nt)
    out[...] = times(terms, 2, dot)


def collision_part(place, kept, sent, factor_high, factor_low):
    shape = (kept.shape[0] // 4, MOMENTS)
    operands = (place, kept, exchanged(sent, 1))
    own, to_one, to_two, to_three = small_call(scatter_kernel, "scatter", 4, shape, operands, 1)
    arrived = (along_y(to_two, 2), along_y(to_three, 3), along_y(to_one, 1))
    summed = small_call(add_four_kernel, "add_four", 1, shape, (own, *arrived))
    operands = (summed, exchanged(summed, 2), factor_high, factor_low)
    share = small_call(collision_kernel, "collide", 1, shape, operands, mib=4)
    whole = small_call(add_two_kernel, "add_two", 1, shape, (share, exchanged(share, 2)))
    pieces = [whole] + [along_y(whole, away) for away in (1, 2, 3)]
    return pieces + [exchanged(piece, 1) for piece in pieces]


def relax_kernel(
    place, own, y_1, y_2, y_3, other, z_1, z_2, z_3, kind, moved, high, low,
    out, gathered, turned_high, turned_low, held, leavings,
):
    size = own.shape[0]
    pieces = (((own, y_1, y_2, y_3), place[0]), ((other, z_1, z_2, z_3), 1 - place[0]))
    for group, core in pieces:
        for away, piece in enumerate(group):
            at = core * 4 + (place[1] + (4 - away)) % 4
            gathered[pl.ds(pl.multiple_of(at * size, size), size), :] = piece[...]
    turned_high[...], turned_low[...] = halves(gathered[...].T)
    fluid = [HALF_STEP * (1 - kind[x : x + 1, :]).astype(F32) for x in range(COLUMNS)]
    sends = []
    start = 0
    for count in (1024, 512, 256, 256):
        lines = pl.ds(start, count)
        gains = []
        for core in range(2):
            cells = slice(core * 2 * ROWS, (core + 1) * 2 * ROWS)
            gain = dot(high[lines, :], turned_high[:, cells])
            gain = gain + dot(high[lines, :], turned_low[:, cells])
            gains.append(gain + dot(low[lines, :], turned_high[:, cells]))
        for part in range(count // CHUNK):
            first = start + part * CHUNK
            for x in range(COLUMNS):
                gain = gains[x // 2][
                    part * CHUNK : (part + 1) * CHUNK, x % 2 * ROWS : (x % 2 + 1) * ROWS
                ]
                held[pl.ds(COLUMNS * first + x, CHUNK, stride=COLUMNS), :] = (
                    moved[x, pl.ds(first, CHUNK), :] + fluid[x] * gain
                )
            rows = pl.ds(COLUMNS * first, COLUMNS * CHUNK)
            send = pltpu.make_async_copy(
                held.at[rows], out.at[rows], leavings.at[first // CHUNK]
            )
            send.start()
            sends.append(send)
        start += count
    for send in sends:
        send.wait()


def relax(place, pieces, kind, moved, high, low):
    return pl.pallas_call(
        relax_kernel,
        name="relax",
        in_specs=[SM] + [VM] * 12,
        out_specs=ANY,
        out_shape=jax.ShapeDtypeStruct((PER_DEVICE * COLUMNS, ROWS), F32),
        scratch_shapes=[
            pltpu.VMEM((CELLS, MOMENTS), F32),
            pltpu.VMEM((MOMENTS, CELLS), BF16),
            pltpu.VMEM((MOMENTS, CELLS), BF16),
            pltpu.VMEM((PER_DEVICE * COLUMNS, ROWS), F32),
            pltpu.SemaphoreType.DMA((PER_DEVICE // CHUNK,)),
        ],
        compiler_params=params(22),
        cost_estimate=cost(8 << 30, 16 * MIB),
    )(place, *pieces, kind, moved, high, low)


def on_device(dist, basis, left_factor, right_factor, mixing, next_cell, prev_cell, cell_kind):
    owner = lax.axis_index("vel")
    place = jnp.stack([owner % 2, owner // 4]).astype(jnp.int32)
    speed = ((MIDDLE - owner.astype(F32)) * STEP * RATIO_X).reshape(1)
    flat = dist.reshape(PER_DEVICE * COLUMNS, ROWS)
    to_right, to_left = pack(flat)
    from_left = shifted(to_right, 1)
    from_right = shifted(to_left, -1)

    given = (to_left[0, :8], left_factor, right_factor, mixing)
    factors = staged(gathered_factors, given)
    high, low, turned_high, turned_low = split_basis(basis)
    part, ends = local_part(speed, flat, cell_kind, row_tables(next_cell, prev_cell))
    factors = split_factors(*factors)
    halo = (from_left, from_right)
    (from_left, from_right), factors = lax.optimization_barrier((halo, factors))

    moved, kept, sent = moments_part(
        speed, place, ends, part, from_left, from_right, cell_kind, high, low
    )
    pieces = collision_part(place, kept, sent, *factors)
    out = relax(place, pieces, cell_kind, moved, turned_high, turned_low)
    return out.reshape(dist.shape)


def solution(mesh):
    in_specs = (
        P("vel", "cells", None),
        P(None, "vel"),
        P("vel", None),
        P("vel", None),
        P(None, "vel"),
        P("cells", None),
        P("cells", None),
        P("cells", None),
    )
    out_specs = P("vel", "cells", None)
    return jax.shard_map(
        on_device, mesh=mesh, in_specs=in_specs, out_specs=out_specs, check_vma=False
    )
```

```python
import functools

import jax
import jax.numpy as jnp
from jax import lax
from jax.experimental import pallas as pl
from jax.experimental.pallas import tpu as pltpu
from jax.sharding import PartitionSpec as P

POINTS = 32
STEP = 6.4 / POINTS
MIDDLE = (POINTS - 1) * 0.5
RATIO_X = 0.2
RATIO_Y = 0.12
HALF_STEP = 0.5

COLUMNS = 4
ROWS = 128
PER_DEVICE = 2048
HALF = PER_DEVICE // 2
CHUNK = 256
CHUNK_M = 1024
MOMENTS = 512
RANKS = 1024
F32 = jnp.float32
BF16 = jnp.bfloat16
MIB = 1 << 20
UP = (0, 1, 2, 3)
DOWN = (3, 2, 1, 0)
CELLS = COLUMNS * ROWS


def shifted(x, by):
    size = lax.axis_size("cells")
    return lax.ppermute(x, "cells", [(i, (i + by) % size) for i in range(size)])


def exchanged(x, bit):
    return lax.ppermute(x, "vel", [(i, i ^ bit) for i in range(16)])


def along_y(x, by):
    return lax.ppermute(x, "vel", [(i, (i + 4 * by) % 16) for i in range(16)])


def halves(x):
    high = x.astype(BF16)
    return high, (x - high.astype(F32)).astype(BF16)


def minmod(a, b):
    return jnp.maximum(jnp.minimum(a, b), 0.0) + jnp.minimum(jnp.maximum(a, b), 0.0)


def dot(a, b):
    return jnp.dot(a, b, preferred_element_type=F32)


def dot_nt(a, b):
    return lax.dot_general(a, b, (((1,), (1,)), ((), ())), preferred_element_type=F32)


def column(ref, x, count=CHUNK):
    return ref[pl.ds(x, count, stride=COLUMNS), :]


def params(mib):
    return pltpu.CompilerParams(vmem_limit_bytes=mib * MIB)


def cost(flops, size):
    return pl.CostEstimate(flops=flops, bytes_accessed=size, transcendentals=0)


VM = pl.BlockSpec(memory_space=pltpu.VMEM)
SM = pl.BlockSpec(memory_space=pltpu.SMEM)
ANY = pl.BlockSpec(memory_space=pl.ANY)


def pack_kernel(flat, right, left, held, right_held, left_held, arrivals, leavings):
    steps = HALF // CHUNK
    rows = CHUNK * COLUMNS
    copies = []
    for i in range(steps):
        for half in range(2):
            at = pl.ds((half * steps + i) * rows, rows)
            copies.append(
                pltpu.make_async_copy(flat.at[at], held.at[at], arrivals.at[2 * i + half])
            )
    for copy in copies:
        copy.start()
    sends = []
    for i in range(steps):
        lower = held.at[pl.ds(i * rows, rows)]
        upper = held.at[pl.ds((steps + i) * rows, rows)]
        out = pl.ds(i * CHUNK, CHUNK)
        copies[2 * i].wait()
        right_held[2, out, :] = column(lower, 3)
        left_held[0, out, :] = column(lower, 0)
        left_held[1, out, :] = column(lower, 1)
        copies[2 * i + 1].wait()
        right_held[0, out, :] = column(upper, 3)
        right_held[1, out, :] = column(upper, 2)
        left_held[2, out, :] = column(upper, 0)
        for j, (source, target) in enumerate(((right_held, right), (left_held, left))):
            send = pltpu.make_async_copy(
                source.at[:, out], target.at[:, out], leavings.at[2 * i + j]
            )
            send.start()
            sends.append(send)
    for send in sends:
        send.wait()


def pack(flat):
    out = jax.ShapeDtypeStruct((3, HALF, ROWS), F32)
    return pl.pallas_call(
        pack_kernel,
        name="pack",
        in_specs=[ANY],
        out_specs=[ANY, ANY],
        out_shape=[out, out],
        scratch_shapes=[
            pltpu.VMEM((PER_DEVICE * COLUMNS, ROWS), F32),
            pltpu.VMEM((3, HALF, ROWS), F32),
            pltpu.VMEM((3, HALF, ROWS), F32),
            pltpu.SemaphoreType.DMA((2 * HALF // CHUNK,)),
            pltpu.SemaphoreType.DMA((2 * HALF // CHUNK,)),
        ],
        compiler_params=params(58),
        cost_estimate=cost(1 << 20, 8 * MIB),
    )(flat)


def staged(stage, operands):
    shapes = jax.eval_shape(stage, *operands)
    blank = lambda *_: jax.tree.map(lambda x: jnp.zeros(x.shape, x.dtype), shapes)
    taken = lax.optimization_barrier(jnp.array(True))
    return lax.cond(taken, stage, blank, *operands)


def local_kernel(speed, dist, kind, tables, out, ends):
    step = pl.program_id(0)
    in_upper = step >= HALF // CHUNK
    line = lax.broadcasted_iota(jnp.int32, (CHUNK, ROWS), 0) + step * CHUNK
    along = (line // POINTS) % POINTS
    along = jnp.where(in_upper, POINTS - 1 - along, along)
    courant_y = jnp.abs((along.astype(F32) - MIDDLE) * STEP * RATIO_Y)
    slope_y = 0.5 * (1.0 - courant_y)
    courant_x = speed[0]
    slope_x = 0.5 * (1.0 - courant_x)
    fields = []
    for x in range(COLUMNS):
        here = column(dist, x)
        both = dot(jnp.concatenate(halves(here), axis=1), tables[0, x])
        face = here + slope_y * minmod(here - both[:, :ROWS], both[:, ROWS:] - here)
        behind = dot(jnp.concatenate(halves(face), axis=1), tables[0, x, :, :ROWS])
        fields.append((here, courant_y * (face - behind)))

    def finish(order):
        here = [fields[x][0] for x in order]
        change = [fields[x][1] for x in order]
        fluid = [(1 - kind[x : x + 1, :]).astype(F32) for x in order]
        face_1 = courant_x * (here[1] + slope_x * minmod(here[1] - here[0], here[2] - here[1]))
        face_2 = courant_x * (here[2] + slope_x * minmod(here[2] - here[1], here[3] - here[2]))
        out[order[0]] = here[0] - fluid[0] * change[0]
        out[order[1]] = here[1] - fluid[1] * (change[1] + face_1)
        out[order[2]] = here[2] - fluid[2] * (change[2] + (face_2 - face_1))
        out[order[3]] = here[3] - fluid[3] * (change[3] - face_2)
        ends[0] = here[0]
        ends[1] = here[1] - here[0]
        ends[2] = here[3]
        ends[3] = here[3] - here[2]

    @pl.when(in_upper)
    def _():
        finish((0, 1, 2, 3))

    @pl.when(jnp.logical_not(in_upper))
    def _():
        finish((3, 2, 1, 0))


def local_part(speed, flat, kind, tables):
    steps = PER_DEVICE // CHUNK
    quarter = steps // 4

    def against(i):
        return jnp.where((i >= quarter) & (i < 3 * quarter), 0, 1)

    return pl.pallas_call(
        local_kernel,
        name="local_transport",
        grid=(steps,),
        in_specs=[
            SM,
            pl.BlockSpec((CHUNK * COLUMNS, ROWS), lambda i: (i, 0)),
            VM,
            pl.BlockSpec((1, COLUMNS, 2 * ROWS, 2 * ROWS), lambda i: (against(i), 0, 0, 0)),
        ],
        out_specs=[pl.BlockSpec((COLUMNS, CHUNK, ROWS), lambda i: (0, i, 0))] * 2,
        out_shape=[jax.ShapeDtypeStruct((COLUMNS, PER_DEVICE, ROWS), F32)] * 2,
        compiler_params=params(14),
        cost_estimate=cost(4 << 30, 10 * MIB),
    )(speed, flat, kind, tables)


def row_tables(following, preceding):
    rows = jnp.arange(ROWS, dtype=jnp.int32)[None, :, None]
    after = (rows == following[:, None, :]).astype(BF16)
    before = (rows == preceding[:, None, :]).astype(BF16)
    forward = jnp.concatenate([before, after], axis=2)
    backward = jnp.concatenate([after, before], axis=2)
    forward = jnp.concatenate([forward, forward], axis=1)
    backward = jnp.concatenate([backward, backward], axis=1)
    return jnp.stack([forward, backward])


def basis_kernel(basis, high, low, turned_high, turned_low):
    values = basis[...]
    high[...], low[...] = halves(values)
    turned_high[...], turned_low[...] = halves(values.T)


def split_basis(basis):
    width = 256
    half = HALF // width
    run = CHUNK_M // width

    def paired(i):
        return (i % half) // run * (2 * run) + i // half * run + i % run

    flat = pl.BlockSpec((MOMENTS, width), lambda i: (0, i))
    ordered = pl.BlockSpec((MOMENTS, width), lambda i: (0, paired(i)))
    turned = pl.BlockSpec((width, MOMENTS), lambda i: (i, 0))
    return pl.pallas_call(
        basis_kernel,
        name="split_basis",
        grid=(PER_DEVICE // width,),
        in_specs=[flat],
        out_specs=[ordered, ordered, turned, turned],
        out_shape=[jax.ShapeDtypeStruct((MOMENTS, PER_DEVICE), BF16)] * 2
        + [jax.ShapeDtypeStruct((PER_DEVICE, MOMENTS), BF16)] * 2,
        compiler_params=params(8),
        cost_estimate=cost(1 << 24, 12 * MIB),
    )(basis)


def stack_kernel(left, right, mixing, out):
    out[:128] = left[...]
    out[128:256] = right[...]
    out[256:] = mixing[...].T


def join_kernel(own, before, after, across_top, across_rest, out):
    out[0] = own[...]
    out[1] = before[...]
    out[2] = after[...]
    out[3, :192] = across_top[...]
    out[3, 192:] = across_rest[...]


def split_kernel(mine, theirs, high, low):
    for i, source in enumerate((mine, theirs)):
        for j in range(4):
            rows = pl.ds((4 * i + j) * 128, 128)
            for which in range(3):
                top, rest = halves(source[j, which * 128 : (which + 1) * 128])
                high[which, rows, :] = top
                low[which, rows, :] = rest


def gathered_factors(_, left, right, mixing):
    own = pl.pallas_call(
        stack_kernel,
        name="stack_factors",
        in_specs=[VM] * 3,
        out_specs=VM,
        out_shape=jax.ShapeDtypeStruct((384, MOMENTS), F32),
        compiler_params=params(3),
        cost_estimate=cost(1 << 20, 2 * MIB),
    )(left, right, mixing)
    before, after = along_y(own, 1), along_y(own, -1)
    across_top, across_rest = along_y(before[:192], 1), along_y(after[192:], -1)
    mine = pl.pallas_call(
        join_kernel,
        name="join_factors",
        in_specs=[VM] * 5,
        out_specs=VM,
        out_shape=jax.ShapeDtypeStruct((4, 384, MOMENTS), F32),
        compiler_params=params(8),
        cost_estimate=cost(1 << 20, 6 * MIB),
    )(own, before, after, across_top, across_rest)
    return mine, exchanged(mine, 1)


def split_factors(mine, theirs):
    out = jax.ShapeDtypeStruct((3, RANKS, MOMENTS), BF16)
    return pl.pallas_call(
        split_kernel,
        name="split_factors",
        in_specs=[VM] * 2,
        out_specs=[VM] * 2,
        out_shape=[out, out],
        compiler_params=params(16),
        cost_estimate=cost(1 << 24, 12 * MIB),
    )(mine, theirs)


def share_of_moments(high, low, values, total, out):
    step = pl.program_id(0)

    @pl.when(step == 0)
    def _():
        total[...] = jnp.zeros_like(total)

    top, rest = halves(values)
    lines = pl.ds(pl.multiple_of(step * (2 * CHUNK_M), 2 * CHUNK_M), 2 * CHUNK_M)
    added = total[...] + dot(high[:, lines], top)
    added = added + dot(high[:, lines], rest)
    added = added + dot(low[:, lines], top)
    total[...] = added

    @pl.when(step == pl.num_programs(0) - 1)
    def _():
        out[...] = total[...].T


def lines_of(which):
    step = pl.program_id(0)
    return pl.ds(pl.multiple_of(which * HALF + step * CHUNK_M, CHUNK_M), CHUNK_M)


def faces_kernel(
    speed, place, ends, part, from_left, from_right, kind, high, low, moved, sent, total
):
    courant = speed[0]
    slope = 0.5 * (1.0 - courant)
    first_core = place[0] == 0

    def half(which, order, behind, behind_two, ahead):
        lines = lines_of(which)
        fluid = [courant * (1 - kind[x : x + 1, :]).astype(F32) for x in order]
        first, forward, fourth, back = (ends[i, lines, :] for i in range(4))
        step_in = first - behind
        face_in = behind + slope * minmod(behind - behind_two, step_in)
        face_0 = first + slope * minmod(step_in, forward)
        face_3 = fourth + slope * minmod(back, ahead - fourth)
        values = {
            order[0]: part[order[0], lines, :] - fluid[0] * (face_0 - face_in),
            order[1]: part[order[1], lines, :] + fluid[1] * face_0,
            order[2]: part[order[2], lines, :],
            order[3]: part[order[3], lines, :] - fluid[3] * face_3,
        }
        for x in range(COLUMNS):
            moved[x, lines, :] = values[x]
        pair = [jnp.where(first_core, values[2 + i], values[i]) for i in range(2)]
        return jnp.concatenate(pair, axis=1)

    left, right, at = from_left, from_right, lines_of(0)
    lower = half(0, DOWN, right[0, at, :], right[1, at, :], left[2, at, :])
    upper = half(1, UP, left[0, at, :], left[1, at, :], right[2, at, :])
    share_of_moments(high, low, jnp.concatenate([lower, upper], axis=0), total, sent)


def moments_kernel(place, moved, high, low, kept, total):
    own = 2 * place[0]
    values = [
        jnp.concatenate([moved[own + i, lines_of(which), :] for i in range(2)], axis=1)
        for which in range(2)
    ]
    share_of_moments(high, low, jnp.concatenate(values, axis=0), total, kept)


def moments_part(speed, place, ends, part, from_left, from_right, kind, high, low):
    piece = jax.ShapeDtypeStruct((CELLS // 2, MOMENTS), F32)
    scratch = [pltpu.VMEM((MOMENTS, CELLS // 2), F32)]
    moved, sent = pl.pallas_call(
        faces_kernel,
        name="faces_and_moments",
        grid=(HALF // CHUNK_M,),
        in_specs=[SM, SM] + [VM] * 7,
        out_specs=[VM] * 2,
        out_shape=[jax.ShapeDtypeStruct((COLUMNS, PER_DEVICE, ROWS), F32), piece],
        scratch_shapes=scratch,
        compiler_params=params(8),
        cost_estimate=cost(4 << 30, 18 * MIB),
    )(speed, place, ends, part, from_left, from_right, kind, high, low)
    kept = pl.pallas_call(
        moments_kernel,
        name="own_moments",
        grid=(HALF // CHUNK_M,),
        in_specs=[SM] + [VM] * 3,
        out_specs=VM,
        out_shape=piece,
        scratch_shapes=scratch,
        compiler_params=params(6),
        cost_estimate=cost(4 << 30, 8 * MIB),
    )(place, moved, high, low)
    return moved, kept, sent


def small_call(kernel, name, count, shape, operands, smem=0, mib=3):
    out = [jax.ShapeDtypeStruct(shape, F32)] * count
    return pl.pallas_call(
        kernel,
        name=name,
        in_specs=[SM] * smem + [VM] * (len(operands) - smem),
        out_specs=[VM] * count if count > 1 else VM,
        out_shape=out if count > 1 else out[0],
        compiler_params=params(mib),
        cost_estimate=cost(1 << 20, 1 * MIB),
    )(*operands)


def scatter_kernel(place, kept, received, own, to_one, to_two, to_three):
    size = own.shape[0]
    for away, out in enumerate((own, to_one, to_two, to_three)):
        at = pl.multiple_of(((place[1] + away) % 4) * size, size)
        out[...] = kept[pl.ds(at, size), :] + received[pl.ds(at, size), :]


def add_four_kernel(a, b, c, d, out):
    out[...] = (a[...] + b[...]) + (c[...] + d[...])


def add_two_kernel(a, b, out):
    out[...] = a[...] + b[...]


def collision_kernel(mine, theirs, high, low, out):
    size = out.shape[0]

    def times(values, which, product):
        top, rest = halves(values)
        both = product(jnp.concatenate([top, rest], axis=0), high[which])
        return both[:size] + (both[size:] + product(top, low[which]))

    moments = mine[...] + theirs[...]
    terms = times(moments, 0, dot_nt) * times(moments, 1, dot_nt)
    out[...] = times(terms, 2, dot)


def collision_part(place, kept, sent, factor_high, factor_low):
    shape = (kept.shape[0] // 4, MOMENTS)
    operands = (place, kept, exchanged(sent, 1))
    own, to_one, to_two, to_three = small_call(scatter_kernel, "scatter", 4, shape, operands, 1)
    arrived = (along_y(to_two, 2), along_y(to_three, 3), along_y(to_one, 1))
    summed = small_call(add_four_kernel, "add_four", 1, shape, (own, *arrived))
    operands = (summed, exchanged(summed, 2), factor_high, factor_low)
    share = small_call(collision_kernel, "collide", 1, shape, operands, mib=4)
    whole = small_call(add_two_kernel, "add_two", 1, shape, (share, exchanged(share, 2)))
    pieces = [whole] + [along_y(whole, away) for away in (1, 2, 3)]
    return pieces + [exchanged(piece, 1) for piece in pieces]


def relax_kernel(
    place, own, y_1, y_2, y_3, other, z_1, z_2, z_3, kind, moved, high, low,
    out, gathered_high, gathered_low, held, leavings,
):
    size = own.shape[0]
    pieces = (((own, y_1, y_2, y_3), place[0]), ((other, z_1, z_2, z_3), 1 - place[0]))
    for group, core in pieces:
        for away, piece in enumerate(group):
            at = core * 4 + (place[1] + (4 - away)) % 4
            rows = pl.ds(pl.multiple_of(at * size, size), size)
            gathered_high[rows, :], gathered_low[rows, :] = halves(piece[...])
    fluid = [HALF_STEP * (1 - kind[x : x + 1, :]).astype(F32) for x in range(COLUMNS)]
    sends = []
    start = 0
    for count in (1024, 512, 256, 256):
        lines = pl.ds(start, count)
        gains = []
        for core in range(2):
            cells = slice(core * 2 * ROWS, (core + 1) * 2 * ROWS)
            gain = dot_nt(high[lines, :], gathered_high[cells, :])
            gain = gain + dot_nt(high[lines, :], gathered_low[cells, :])
            gains.append(gain + dot_nt(low[lines, :], gathered_high[cells, :]))
        for part in range(count // CHUNK):
            first = start + part * CHUNK
            for x in range(COLUMNS):
                gain = gains[x // 2][
                    part * CHUNK : (part + 1) * CHUNK, x % 2 * ROWS : (x % 2 + 1) * ROWS
                ]
                held[pl.ds(COLUMNS * first + x, CHUNK, stride=COLUMNS), :] = (
                    moved[x, pl.ds(first, CHUNK), :] + fluid[x] * gain
                )
            rows = pl.ds(COLUMNS * first, COLUMNS * CHUNK)
            send = pltpu.make_async_copy(
                held.at[rows], out.at[rows], leavings.at[first // CHUNK]
            )
            send.start()
            sends.append(send)
        start += count
    for send in sends:
        send.wait()


def relax(place, pieces, kind, moved, high, low):
    return pl.pallas_call(
        relax_kernel,
        name="relax",
        in_specs=[SM] + [VM] * 12,
        out_specs=ANY,
        out_shape=jax.ShapeDtypeStruct((PER_DEVICE * COLUMNS, ROWS), F32),
        scratch_shapes=[
            pltpu.VMEM((CELLS, MOMENTS), BF16),
            pltpu.VMEM((CELLS, MOMENTS), BF16),
            pltpu.VMEM((PER_DEVICE * COLUMNS, ROWS), F32),
            pltpu.SemaphoreType.DMA((PER_DEVICE // CHUNK,)),
        ],
        compiler_params=params(22),
        cost_estimate=cost(8 << 30, 16 * MIB),
    )(place, *pieces, kind, moved, high, low)


def on_device(dist, basis, left_factor, right_factor, mixing, next_cell, prev_cell, cell_kind):
    owner = lax.axis_index("vel")
    place = jnp.stack([owner % 2, owner // 4]).astype(jnp.int32)
    speed = ((MIDDLE - owner.astype(F32)) * STEP * RATIO_X).reshape(1)
    flat = dist.reshape(PER_DEVICE * COLUMNS, ROWS)
    to_right, to_left = pack(flat)
    from_right = shifted(to_left, -1)
    from_left = shifted(to_right, 1)

    given = (to_left[0, :8], left_factor, right_factor, mixing)
    factors = staged(gathered_factors, given)
    high, low, turned_high, turned_low = split_basis(basis)
    part, ends = local_part(speed, flat, cell_kind, row_tables(next_cell, prev_cell))
    factors = split_factors(*factors)
    halo = (from_right, from_left)
    (from_right, from_left), factors = lax.optimization_barrier((halo, factors))

    moved, kept, sent = moments_part(
        speed, place, ends, part, from_left, from_right, cell_kind, high, low
    )
    pieces = collision_part(place, kept, sent, *factors)
    out = relax(place, pieces, cell_kind, moved, turned_high, turned_low)
    return out.reshape(dist.shape)


def solution(mesh):
    in_specs = (
        P("vel", "cells", None),
        P(None, "vel"),
        P("vel", None),
        P("vel", None),
        P(None, "vel"),
        P("cells", None),
        P("cells", None),
        P("cells", None),
    )
    out_specs = P("vel", "cells", None)
    return jax.shard_map(
        on_device, mesh=mesh, in_specs=in_specs, out_specs=out_specs, check_vma=False
    )
```
